512 devices in a mesh: ulysses: 8 (over x, y_lo), blk: 8 (over z), tensor: 8 (over y_hi, core).
Axes of the slice: x: 4, y: 8 (y_hi: 4, y_lo: 2; y = y_hi * 2 + y_lo), z: 8, core: 2. Of those that a mesh axis runs over, the one named last changes fastest.
Arguments:
- tokens: bfloat16 [4096, 3072], P(('ulysses', 'blk'), 'tensor'), may hold values from -12 to 12
- cond: bfloat16 [3072], replicated, may hold values from -4 to 4
- mod_weight: bfloat16 [3072, 18432], P(None, ('ulysses', 'blk', 'tensor')), may hold values from -0.109375 to 0.109375
- qkv_weight: bfloat16 [3072, 3, 3072], P('tensor', None, 'ulysses'), as said below
- q_gain: float32 [128], replicated, may hold values from 1.2 to 3.4, as said below
- k_gain: float32 [128], replicated, may hold values from 1.2 to 3.4, as said below
- out_weight: bfloat16 [3072, 3072], P('ulysses', 'tensor'), may hold values from -0.109375 to 0.109375
- up_weight: bfloat16 [3072, 12288], P('tensor', 'ulysses'), may hold values from -0.109375 to 0.109375
- down_weight: bfloat16 [12288, 3072], P('ulysses', 'tensor'), may hold values from -0.0546875 to 0.0546875
Outputs:
- block_out: float32 [4096, 3072], P(('ulysses', 'blk'), 'tensor')
The draws below stay inside these ranges and needn't reach their ends.
Inputs may be any that keep to these rules, and one draw needn't show every extreme that they name: `qkv_weight`: entries lie within four times 3072 ** -0.5 of zero. `q_gain`: positive gains. `k_gain`: positive gains.
All inputs are finite; a program needn't handle non-finite values.
Results may differ from the reference program's by a relative error of at most 0.011.
Values may be sent and summed in bfloat16 or wider, within the bound.
A program may use at most 64 MiB of HBM per device.

```python
import math
import jax
import jax.numpy as jnp
from jax import lax

D = 3072
HEADS = 24
HEAD = 128
FF = 12288
TOKENS = 4096
N_ULYSSES = 8
N_TENSOR = 8


def draw_tokens(key, part):
    key = jax.random.fold_in(key, 11)
    first, second, third = jax.random.split(key, 3)
    column_pos = jnp.arange(D, dtype=jnp.float32) / D
    column_scale = jnp.power(3.0, column_pos) / math.sqrt(3.0) * jnp.power(10.0, jax.random.uniform(second, (D,), minval=-0.15, maxval=0.15))
    row_scale = jnp.power(10.0, jax.random.uniform(third, (TOKENS, 1), minval=-0.15, maxval=0.15))
    base = jax.random.truncated_normal(first, -2.8, 2.8, (TOKENS, D))
    return (base * row_scale * column_scale).astype(jnp.bfloat16)


def draw_qkv_weight(key, part):
    key = jax.random.fold_in(key, 12)
    weights = jax.random.truncated_normal(key, -4.0, 4.0, (D, 3, HEADS * HEAD)) / math.sqrt(D)
    return weights.astype(jnp.bfloat16)


def draw_q_gain(key, part):
    key = jax.random.fold_in(key, 13)
    gains = jax.random.uniform(key, (HEAD,), minval=1.2, maxval=2.2)
    return gains.astype(jnp.float32)


def draw_k_gain(key, part):
    key = jax.random.fold_in(key, 14)
    gains = jax.random.uniform(key, (HEAD,), minval=1.2, maxval=2.2)
    return gains.astype(jnp.float32)


def block_levels(own_key, dims, cuts, smallest, largest):
    def one(position, parts):
        steps = jax.random.uniform(jax.random.fold_in(jax.random.fold_in(own_key, 6), position), (parts,), jnp.float32, smallest / len(cuts), largest / len(cuts))
        return jnp.repeat(jnp.exp(steps), dims[position] // parts).reshape((-1,) + (1,) * (len(dims) - position - 1))

    level = one(*cuts[0])
    for cut in cuts[1:]:
        level = level * one(*cut)
    return level


def scatter_about(own_key, extent, deviation, most, cuts=(), kind=jnp.bfloat16):
    factor_of = block_levels(own_key, extent, cuts, -0.22, 0.18) if cuts else 1.0
    entries = jax.random.normal(own_key, extent, jnp.float32) * deviation * factor_of
    return jnp.minimum(jnp.maximum(entries, -most), most).astype(kind)


def setup_inputs(seed: int = 0) -> dict:
    key_list = jax.random.split(jax.random.key(seed), 10)
    tokens = draw_tokens(jax.random.fold_in(key_list[9], 71), 0)
    cond = scatter_about(key_list[1], (D,), 1.0, 4.0)
    mod_weight = scatter_about(key_list[2], (D, 6 * D), D ** -0.5, 0.109375, ((1, 512),))
    qkv_weight = draw_qkv_weight(jax.random.fold_in(key_list[9], 71), 0)
    q_gain = draw_q_gain(jax.random.fold_in(key_list[9], 71), 0)
    k_gain = draw_k_gain(jax.random.fold_in(key_list[9], 71), 0)
    out_weight = scatter_about(key_list[6], (HEADS * HEAD, D), (HEADS * HEAD) ** -0.5, 0.109375, ((0, 8), (1, 8)))
    up_weight = scatter_about(key_list[7], (D, FF), D ** -0.5, 0.109375, ((0, 8), (1, 8)))
    down_weight = scatter_about(key_list[8], (FF, D), FF ** -0.5, 0.0546875, ((0, 8), (1, 8)))
    return {"tokens": tokens, "cond": cond, "mod_weight": mod_weight, "qkv_weight": qkv_weight, "q_gain": q_gain, "k_gain": k_gain, "out_weight": out_weight, "up_weight": up_weight, "down_weight": down_weight}


def layer_norm(values):
    center = values - lax.optimization_barrier(jnp.mean(values, axis=-1, keepdims=True))
    variance = lax.optimization_barrier(jnp.mean(center * center, axis=-1, keepdims=True))
    return center * lax.rsqrt(variance + 1e-06)

def head_norm(values, gains):
    return values * lax.rsqrt(lax.optimization_barrier(jnp.mean(values * values, axis=-1, keepdims=True)) + 1e-06) * gains

def rounded(values):
    return lax.optimization_barrier(values.astype(jnp.bfloat16)).astype(jnp.float32)

def grouped_product(left, right, groups):
    width = left.shape[1] // groups
    result = jnp.zeros((left.shape[0], right.shape[1]), jnp.float32)
    for group in range(groups):
        partial_product = jnp.dot(left[:, group * width:(group + 1) * width], right[group * width:(group + 1) * width], preferred_element_type=jnp.float32)
        result = result + rounded(partial_product)
    return result

def reference(tokens, cond, mod_weight, qkv_weight, q_gain, k_gain, out_weight, up_weight, down_weight):
    activated = jax.nn.silu(cond.astype(jnp.float32)).astype(jnp.bfloat16)
    modulation = jnp.dot(activated[None, :], mod_weight, preferred_element_type=jnp.float32)[0].reshape(6, D)
    resid = tokens.astype(jnp.float32)
    normed = (layer_norm(resid) * (1.0 + modulation[1]) + modulation[0]).astype(jnp.bfloat16)
    inner = HEADS * HEAD
    projected = grouped_product(normed, qkv_weight.reshape(D, 3 * inner), N_TENSOR)
    projected = projected.reshape(TOKENS, 3, HEADS, HEAD)
    queries = head_norm(projected[:, 0], q_gain).astype(jnp.bfloat16)
    keys = head_norm(projected[:, 1], k_gain).astype(jnp.bfloat16)
    values = projected[:, 2].astype(jnp.bfloat16)
    score_scale = 1.0 / math.sqrt(HEAD)

    def one_head(operands):
        head_query, head_key, head_value = operands
        scores = jnp.dot(head_query, head_key.T, preferred_element_type=jnp.float32) * score_scale
        weights = jnp.exp(scores - lax.optimization_barrier(jnp.max(scores, axis=-1, keepdims=True)))
        denominator = lax.optimization_barrier(jnp.sum(weights, axis=-1, keepdims=True))
        summed = jnp.dot(weights.astype(jnp.bfloat16), head_value, preferred_element_type=jnp.float32)
        return (summed / denominator).astype(jnp.bfloat16)
    context = lax.map(one_head, (jnp.moveaxis(queries, 1, 0), jnp.moveaxis(keys, 1, 0), jnp.moveaxis(values, 1, 0)))
    context = jnp.moveaxis(context, 0, 1).reshape(TOKENS, inner)
    attended = grouped_product(context, out_weight, N_ULYSSES)
    mixed = resid + modulation[2] * attended
    normed_two = (layer_norm(mixed) * (1.0 + modulation[4]) + modulation[3]).astype(jnp.bfloat16)
    hidden = grouped_product(normed_two, up_weight, N_TENSOR)
    activ = jax.nn.gelu(hidden, approximate=True).astype(jnp.bfloat16)
    feedforward = grouped_product(activ, down_weight, N_ULYSSES)
    return mixed + modulation[5] * feedforward
```

```python
import functools
import math

import jax
import jax.numpy as jnp
from jax import lax
from jax.experimental import pallas as pl
from jax.experimental.pallas import tpu as pltpu
from jax.sharding import PartitionSpec as P

MESH = pl.DeviceIdType.MESH
F32 = jnp.float32
BF16 = jnp.bfloat16


def block_kernel(
    U, B, T,
    tokens, cond, mod_w, qkv_w, q_gain, k_gain, out_w, up_w, down_w,
    out,
    tok_own, tok_rx, mw, wq, wo, wu, wd,
    m_tx, m_a, m_d, m_b, m_u, m_c, modv,
    st_tx, st_rx, rs_tx, rs_rx, q_rx, kv_rx, o_tx, o_rx, ctx_rx,
    at_tx, at_rx, mix, s2_tx, s2_rx, n2_tx, n2_rx, up_tx, up_rx, act_rx, ff_tx, ff_rx,
    loc_sem, w_send, w_recv,
    tok_send, tok_recv, ma_send, ma_recv, mb_send, mb_recv, mc_send, mc_recv,
    st_send, st_recv, rs_send, rs_recv, q_send, q_recv, kv_send, kv_recv, o_send, o_recv,
    cx_send, cx_recv, at_send, at_recv, s2_send, s2_recv, n2_send, n2_recv,
    up_send, up_recv, ac_send, ac_recv, ff_send, ff_recv,
):
    C = 2
    H = T // C
    R, W = tokens.shape
    G = H * R
    features = W * T
    u = lax.axis_index("ulysses")
    b = lax.axis_index("blk")
    t = lax.axis_index("tensor")
    h = t // C
    c = lax.rem(t, C)
    mate = {"tensor": h * C + (1 - c)}
    uc = u // H
    ui = lax.rem(u, H)
    pending = []
    y_far = sorted(range(1, H), key=lambda k: -min(k, H - k))
    y_near = y_far[::-1]

    def rdma(src, dst, send, recv, dev):
        copy = pltpu.make_async_remote_copy(
            src_ref=src, dst_ref=dst, send_sem=send, recv_sem=recv,
            device_id=dev, device_id_type=MESH,
        )
        copy.start()
        pending.append((None, copy))

    def rdma_or_local(own, src, dst, send, recv, dev):
        copy = pltpu.make_async_remote_copy(
            src_ref=src, dst_ref=dst, send_sem=send, recv_sem=recv,
            device_id=dev, device_id_type=MESH,
        )

        @pl.when(own)
        def _():
            pltpu.make_async_copy(src, dst, recv).start()

        @pl.when(jnp.logical_not(own))
        def _():
            copy.start()

        pending.append((own, copy))

    def arrived(dst, recv):
        pltpu.make_async_copy(dst, dst, recv).wait()

    def y_peer(k):
        hp = lax.rem(h + k, H)
        return hp, {"tensor": hp * C + c}

    barrier = pltpu.get_barrier_semaphore()
    count = 0
    for k in range(1, B):
        pl.semaphore_signal(barrier, inc=1, device_id={"blk": lax.rem(b + k, B)}, device_id_type=MESH)
        count += 1
    for k in range(1, T):
        pl.semaphore_signal(barrier, inc=1, device_id={"tensor": lax.rem(t + k, T)}, device_id_type=MESH)
        count += 1
    for k in range(1, U):
        for cc in range(C):
            pl.semaphore_signal(
                barrier, inc=1,
                device_id={"ulysses": lax.rem(u + k, U), "tensor": h * C + cc},
                device_id_type=MESH,
            )
            count += 1

    local = [
        pltpu.make_async_copy(mod_w, mw, loc_sem.at[0]),
        pltpu.make_async_copy(tokens, tok_own, loc_sem.at[1]),
        pltpu.make_async_copy(qkv_w, wq.at[:, c], loc_sem.at[2]),
        pltpu.make_async_copy(out_w, wo.at[c], loc_sem.at[3]),
        pltpu.make_async_copy(up_w, wu.at[c], loc_sem.at[4]),
        pltpu.make_async_copy(down_w, wd.at[c], loc_sem.at[5]),
    ]
    for copy in local:
        copy.start()

    condf = cond[...].astype(F32)
    active = (condf * jax.nn.sigmoid(condf)).astype(BF16)
    local[0].wait()
    share = lax.dot_general(
        jnp.broadcast_to(active, (16, features)), mw[...],
        (((1,), (1,)), ((), ())), preferred_element_type=F32,
    )
    n_share = mod_w.shape[0]
    start = n_share * (b * T + t)
    lanes2 = lax.broadcasted_iota(jnp.int32, (n_share, 256), 1)
    rows2 = lax.broadcasted_iota(jnp.int32, (n_share, 256), 0)
    place = (lanes2 == rows2 + lax.rem(start, 128)).astype(F32)
    placed = jnp.dot(share[0:8], place, preferred_element_type=F32, precision=lax.Precision.HIGHEST)
    sub8 = lax.broadcasted_iota(jnp.int32, (8, 128), 0)
    tile = jnp.where(sub8 == 0, placed[:, 0:128], jnp.where(sub8 == 1, placed[:, 128:256], 0.0))
    m_tx[...] = tile
    m_a[b] = tile

    pl.semaphore_wait(barrier, count)

    for k in range(1, B):
        rdma(m_tx, m_a.at[b], ma_send.at[k], ma_recv.at[b], {"blk": lax.rem(b + k, B)})
    for up_ in range(U):
        rdma_or_local(
            jnp.logical_and(u == up_, c == uc),
            tokens, tok_rx.at[c, pl.ds(ui * R, R), :], tok_send.at[up_], tok_recv.at[c, ui],
            {"ulysses": up_, "tensor": h * C + uc},
        )
    rdma(qkv_w, wq.at[:, c], w_send.at[0], w_recv.at[0], mate)
    rdma(out_w, wo.at[c], w_send.at[1], w_recv.at[1], mate)
    rdma(up_w, wu.at[c], w_send.at[2], w_recv.at[2], mate)
    rdma(down_w, wd.at[c], w_send.at[3], w_recv.at[3], mate)

    per_u = n_share * B * T // 128
    m_d[...] = jnp.zeros_like(m_d)
    for k in range(B):
        if k:
            bp = lax.rem(b + k, B)
            arrived(m_a.at[bp], ma_recv.at[bp])
    for bp in range(B):
        row = (n_share * (bp * T + t)) // 128
        m_d[pl.ds(row, 1), :] += m_a[bp, 0:1, :]
        m_d[pl.ds(row + 1, 1), :] += m_a[bp, 1:2, :]
    m_b[t] = m_d[...]
    for k in range(1, T):
        rdma(m_d, m_b.at[t], mb_send.at[k], mb_recv.at[t], {"tensor": lax.rem(t + k, T)})

    for cc in range(C):
        for i in range(H):
            arrived(tok_rx.at[cc, pl.ds(i * R, R), :], tok_recv.at[cc, i])
    x0 = tok_rx[0].astype(F32)
    x1 = tok_rx[1].astype(F32)
    local_mean = (jnp.sum(x0, -1, keepdims=True) + jnp.sum(x1, -1, keepdims=True)) * (1.0 / (C * W))
    d0 = x0 - local_mean
    d1 = x1 - local_mean
    local_m2 = jnp.sum(d0 * d0, -1, keepdims=True) + jnp.sum(d1 * d1, -1, keepdims=True)
    lane = lax.broadcasted_iota(jnp.int32, (G, 128), 1)
    stats = jnp.where(lane == 0, local_mean, jnp.where(lane == 1, local_m2, 0.0))
    stats_t = jnp.transpose(stats)[0:8]
    st_tx[...] = stats_t
    st_rx[h] = stats_t
    for k in range(1, H):
        hp, dev = y_peer(k)
        rdma(st_tx, st_rx.at[h], st_send.at[k], st_recv.at[h], dev)

    for k in range(1, T):
        tp = lax.rem(t + k, T)
        arrived(m_b.at[tp], mb_recv.at[tp])
    dense = m_b[0]
    for tp in range(1, T):
        dense = dense + m_b[tp]
    m_u[...] = dense
    m_c[u] = dense
    for k in range(1, U):
        rdma(m_u, m_c.at[u], mc_send.at[k], mc_recv.at[u], {"ulysses": lax.rem(u + k, U)})

    for k in range(1, H):
        hp, _ = y_peer(k)
        arrived(st_rx.at[hp], st_recv.at[hp])
    mean = st_rx[0, 0:1, :]
    for hp in range(1, H):
        mean = mean + st_rx[hp, 0:1, :]
    mean = mean * (1.0 / H)
    m2 = jnp.zeros_like(mean)
    for hp in range(H):
        diff = st_rx[hp, 0:1, :] - mean
        m2 = m2 + st_rx[hp, 1:2, :] + (C * W) * diff * diff
    rstd = lax.rsqrt(m2 * (1.0 / features) + 1e-06)
    subg = lax.broadcasted_iota(jnp.int32, (128, G), 0)
    cols = jnp.transpose(jnp.where(subg == 0, mean, jnp.where(subg == 1, rstd, 0.0)))
    mean_c, rstd_c = cols[:, 0:1], cols[:, 1:2]

    for k in range(1, U):
        upk = lax.rem(u + k, U)
        arrived(m_c.at[upk], mc_recv.at[upk])
    for v in range(6):
        for k in range(C * W // 128):
            row = v * (features // 128) + h * (C * W // 128) + k
            modv[v:v + 1, 128 * k:128 * (k + 1)] = m_c[row // per_u, pl.ds(lax.rem(row, per_u), 1), :]

    n0 = ((x0 - mean_c) * rstd_c * (1.0 + modv[1:2, 0:W]) + modv[0:1, 0:W]).astype(BF16)
    n1 = ((x1 - mean_c) * rstd_c * (1.0 + modv[1:2, W:2 * W]) + modv[0:1, W:2 * W]).astype(BF16)

    local[2].wait()
    arrived(wq.at[:, 1 - c], w_recv.at[0])
    for g in range(3):
        part = jnp.dot(n0, wq[g, 0], preferred_element_type=F32)
        part = part + jnp.dot(n1, wq[g, 1], preferred_element_type=F32)
        rs_tx[g] = part.astype(BF16)
        for k in y_far:
            hp, dev = y_peer(k)
            rdma(rs_tx.at[g, pl.ds(hp * R, R), :], rs_rx.at[g, h], rs_send.at[g, k], rs_recv.at[g, h], dev)
        rs_rx[g, h] = rs_tx[g, pl.ds(h * R, R), :]

    slot = c * H + h
    heads = W // 128
    for g in range(3):
        for k in y_near:
            hp, _ = y_peer(k)
            arrived(rs_rx.at[g, hp], rs_recv.at[g, hp])
        total = rs_rx[g, 0].astype(F32)
        for hp in range(1, H):
            total = total + rs_rx[g, hp].astype(F32)
        if g < 2:
            gain = (q_gain if g == 0 else k_gain)[...]
            pieces = []
            for hd in range(heads):
                piece = total[:, 128 * hd:128 * (hd + 1)]
                ms = jnp.mean(piece * piece, axis=-1, keepdims=True)
                pieces.append(piece * lax.rsqrt(ms + 1e-06) * gain)
            total = jnp.concatenate(pieces, axis=1)
        if g == 0:
            q_rx[pl.ds(b * R, R), :] = total.astype(BF16)
            for k in range(1, B):
                rows = q_rx.at[pl.ds(b * R, R), :]
                rdma(rows, rows, q_send.at[k], q_recv.at[b], {"blk": lax.rem(b + k, B)})
        else:
            rows = kv_rx.at[g - 1, pl.ds(slot * R, R), :]
            kv_rx[g - 1, pl.ds(slot * R, R), :] = total.astype(BF16)
            for k in y_far:
                _, dev = y_peer(k)
                rdma(rows, rows, kv_send.at[g - 1, k], kv_recv.at[g - 1, slot], dev)
            rdma(rows, rows, kv_send.at[g - 1, 0], kv_recv.at[g - 1, slot], mate)
    for g in range(2):
        for k in y_near:
            hp, _ = y_peer(k)
            sp = c * H + hp
            rows = kv_rx.at[g, pl.ds(sp * R, R), :]
            arrived(rows, kv_recv.at[g, sp])
            rdma(rows, rows, kv_send.at[g, 4 + k], kv_recv.at[g, sp], mate)
    for k in range(1, B):
        bp = lax.rem(b + k, B)
        arrived(q_rx.at[pl.ds(bp * R, R), :], q_recv.at[bp])
    for g in range(2):
        for hp in range(H):
            sp = (1 - c) * H + hp
            arrived(kv_rx.at[g, pl.ds(sp * R, R), :], kv_recv.at[g, sp])

    scale = 1.0 / math.sqrt(128)
    QB = 128 if B * R % 128 == 0 else R

    def attend(qb, carry):
        at = pl.multiple_of(qb * QB, QB)
        lane_q = lax.broadcasted_iota(jnp.int32, (QB, 128), 1)
        tail = jnp.zeros((QB, 128), F32)
        for hd in range(heads):
            cut = slice(128 * hd, 128 * (hd + 1))
            s = lax.dot_general(
                q_rx[pl.ds(at, QB), cut], kv_rx[0, :, cut],
                (((1,), (1,)), ((), ())), preferred_element_type=F32,
            )
            top = jnp.max(s, axis=-1, keepdims=True).astype(BF16).astype(F32)
            p = jnp.exp((s - top) * scale)
            weight = jnp.sum(p, axis=-1, keepdims=True)
            o = jnp.dot(p.astype(BF16), kv_rx[1, :, cut], preferred_element_type=F32)
            o_tx[pl.ds(at, QB), cut] = o.astype(BF16)
            high = weight.astype(BF16).astype(F32)
            tail = jnp.where(lane_q == hd, top, tail)
            tail = jnp.where(lane_q == heads + hd, high, tail)
            tail = jnp.where(lane_q == 2 * heads + hd, weight - high, tail)
        o_tx[pl.ds(at, QB), W:W + 128] = tail.astype(BF16)
        return carry

    lax.fori_loop(0, B * R // QB, attend, 0)
    o_rx[b] = o_tx[pl.ds(b * R, R), :]
    for k in sorted(range(1, B), key=lambda k: -min(k, B - k)):
        bp = lax.rem(b + k, B)
        rdma(o_tx.at[pl.ds(bp * R, R), :], o_rx.at[b], o_send.at[k], o_recv.at[b], {"blk": bp})
    for k in range(1, B):
        bp = lax.rem(b + k, B)
        arrived(o_rx.at[bp], o_recv.at[bp])
    pieces = []
    for hd in range(heads):
        cut = slice(128 * hd, 128 * (hd + 1))
        tops = [o_rx[bp, :, W + hd:W + hd + 1].astype(F32) for bp in range(B)]
        top = functools.reduce(jnp.maximum, tops)
        num = jnp.zeros((R, 128), F32)
        den = jnp.zeros((R, 1), F32)
        for bp in range(B):
            share_b = jnp.exp((tops[bp] - top) * scale)
            num = num + share_b * o_rx[bp, :, cut].astype(F32)
            den = den + share_b * (
                o_rx[bp, :, W + heads + hd:W + heads + hd + 1].astype(F32)
                + o_rx[bp, :, W + 2 * heads + hd:W + 2 * heads + hd + 1].astype(F32)
            )
        pieces.append(num / den)
    mine = ctx_rx.at[pl.ds(h * R, R), :]
    ctx_rx[pl.ds(h * R, R), :] = jnp.concatenate(pieces, axis=1).astype(BF16)
    for k in y_far:
        _, dev = y_peer(k)
        rdma(mine, mine, cx_send.at[k], cx_recv.at[h], dev)
    local[3].wait()
    arrived(wo.at[1 - c], w_recv.at[1])
    for k in y_near:
        hp, _ = y_peer(k)
        arrived(ctx_rx.at[pl.ds(hp * R, R), :], cx_recv.at[hp])

    def to_owners(tx, rx, send, recv, cc):
        for hp in range(H):
            up_ = c * H + hp
            rdma_or_local(
                jnp.logical_and(up_ == u, c == cc),
                tx.at[cc, pl.ds(hp * R, R), :], rx.at[u], send.at[cc, hp], recv.at[u],
                {"ulysses": up_, "tensor": h * C + cc},
            )

    for cc in range(C):
        at_tx[cc] = jnp.dot(ctx_rx[...], wo[cc], preferred_element_type=F32).astype(BF16)
        to_owners(at_tx, at_rx, at_send, at_recv, cc)
    for up_ in range(U):
        arrived(at_rx.at[up_], at_recv.at[up_])
    attended = at_rx[0].astype(F32)
    for up_ in range(1, U):
        attended = attended + at_rx[up_].astype(F32)
    local[1].wait()
    own_cols = pl.ds(pl.multiple_of(c * W, 128), W)
    mixed = tok_own[...].astype(F32) + modv[2:3, own_cols] * attended
    mix[...] = mixed

    mean_l = jnp.sum(mixed, -1, keepdims=True) * (1.0 / W)
    diff = mixed - mean_l
    m2_l = jnp.sum(diff * diff, -1, keepdims=True)
    lane_r = lax.broadcasted_iota(jnp.int32, (R, 128), 1)
    st2 = jnp.where(lane_r == 0, mean_l, jnp.where(lane_r == 1, m2_l, 0.0))
    st2_t = jnp.transpose(jnp.concatenate([st2, jnp.zeros((128 - R, 128), F32)], axis=0))[0:8]
    s2_tx[...] = st2_t
    s2_rx[t] = st2_t
    for k in range(1, T):
        rdma(s2_tx, s2_rx.at[t], s2_send.at[k], s2_recv.at[t], {"tensor": lax.rem(t + k, T)})
    for k in range(1, T):
        tp = lax.rem(t + k, T)
        arrived(s2_rx.at[tp], s2_recv.at[tp])
    total = s2_rx[0]
    for tp in range(1, T):
        total = total + s2_rx[tp]
    mean2 = total[0:1] * (1.0 / T)
    m2 = total[1:2]
    for tp in range(T):
        dev2 = s2_rx[tp, 0:1, :] - mean2
        m2 = m2 + W * dev2 * dev2
    rstd2 = lax.rsqrt(m2 * (1.0 / features) + 1e-06)
    sub2 = lax.broadcasted_iota(jnp.int32, (128, 128), 0)
    cols2 = jnp.transpose(jnp.where(sub2 == 0, mean2, jnp.where(sub2 == 1, rstd2, 0.0)))
    normed = (mixed - cols2[0:R, 0:1]) * cols2[0:R, 1:2]
    n2_tx[...] = (normed * (1.0 + modv[4:5, own_cols]) + modv[3:4, own_cols]).astype(BF16)
    for up_ in range(U):
        rdma_or_local(
            jnp.logical_and(u == up_, c == uc),
            n2_tx, n2_rx.at[c, pl.ds(ui * R, R), :], n2_send.at[up_], n2_recv.at[c, ui],
            {"ulysses": up_, "tensor": h * C + uc},
        )
    local[4].wait()
    arrived(wu.at[1 - c], w_recv.at[2])
    for cc in range(C):
        for i in range(H):
            arrived(n2_rx.at[cc, pl.ds(i * R, R), :], n2_recv.at[cc, i])

    J = up_w.shape[1] // W
    for j in range(J):
        cut = slice(W * j, W * (j + 1))
        part = jnp.dot(n2_rx[0], wu[0, :, cut], preferred_element_type=F32)
        part = part + jnp.dot(n2_rx[1], wu[1, :, cut], preferred_element_type=F32)
        up_tx[j] = part.astype(BF16)
        for k in y_far:
            hp, dev = y_peer(k)
            rdma(up_tx.at[j, pl.ds(hp * R, R), :], up_rx.at[j, h], up_send.at[j, k], up_recv.at[j, h], dev)
        up_rx[j, h] = up_tx[j, pl.ds(h * R, R), :]
    for j in range(J):
        for k in y_near:
            hp, _ = y_peer(k)
            arrived(up_rx.at[j, hp], up_recv.at[j, hp])
        hidden = up_rx[j, 0].astype(F32)
        for hp in range(1, H):
            hidden = hidden + up_rx[j, hp].astype(F32)
        mine = act_rx.at[j, pl.ds(h * R, R), :]
        act_rx[j, pl.ds(h * R, R), :] = jax.nn.gelu(hidden, approximate=True).astype(BF16)
        for k in y_far:
            _, dev = y_peer(k)
            rdma(mine, mine, ac_send.at[j, k], ac_recv.at[j, h], dev)
    local[5].wait()
    arrived(wd.at[1 - c], w_recv.at[3])
    accs = [None] * C
    for j in range(J):
        for k in y_near:
            hp, _ = y_peer(k)
            arrived(act_rx.at[j, pl.ds(hp * R, R), :], ac_recv.at[j, hp])
        for cc in range(C):
            part = jnp.dot(act_rx[j], wd[cc, W * j:W * (j + 1), :], preferred_element_type=F32)
            accs[cc] = part if j == 0 else accs[cc] + part
    for cc in range(C):
        ff_tx[cc] = accs[cc].astype(BF16)
        to_owners(ff_tx, ff_rx, ff_send, ff_recv, cc)
    for up_ in range(U):
        arrived(ff_rx.at[up_], ff_recv.at[up_])
    feed = ff_rx[0].astype(F32)
    for up_ in range(1, U):
        feed = feed + ff_rx[up_].astype(F32)
    out[...] = mix[...] + modv[5:6, own_cols] * feed

    for own, copy in pending:
        if own is None:
            copy.wait_send()
        else:
            pl.when(jnp.logical_not(own))(copy.wait_send)


def on_device(
    tokens, cond, mod_weight, qkv_weight, q_gain, k_gain, out_weight, up_weight, down_weight
):
    U = lax.axis_size("ulysses")
    B = lax.axis_size("blk")
    T = lax.axis_size("tensor")
    H = T // 2
    R, W = tokens.shape
    G = H * R
    FFL = up_weight.shape[1]
    J = FFL // W
    dma = pltpu.SemaphoreType.DMA
    vmem = pltpu.VMEM
    any_spec = pl.BlockSpec(memory_space=pl.ANY)
    vm_spec = pl.BlockSpec(memory_space=pltpu.VMEM)
    return pl.pallas_call(
        functools.partial(block_kernel, U, B, T),
        out_shape=jax.ShapeDtypeStruct((R, W), F32),
        in_specs=[any_spec, vm_spec, any_spec, any_spec, vm_spec, vm_spec, any_spec, any_spec, any_spec],
        out_specs=vm_spec,
        scratch_shapes=[
            vmem((R, W), BF16),
            vmem((2, G, W), BF16),
            vmem((mod_weight.shape[1], mod_weight.shape[0]), BF16),
            vmem((3, 2, W, W), BF16),
            vmem((2, W, W), BF16),
            vmem((2, W, FFL), BF16),
            vmem((2, FFL, W), BF16),
            vmem((8, 128), F32),
            vmem((B, 8, 128), F32),
            vmem((24, 128), F32),
            vmem((T, 24, 128), F32),
            vmem((24, 128), F32),
            vmem((U, 24, 128), F32),
            vmem((8, 2 * W), F32),
            vmem((8, G), F32),
            vmem((H, 8, G), F32),
            vmem((3, G, W), BF16),
            vmem((3, H, R, W), BF16),
            vmem((B * R, W), BF16),
            vmem((2, T * R, W), BF16),
            vmem((B * R, W + 128), BF16),
            vmem((B, R, W + 128), BF16),
            vmem((G, W), BF16),
            vmem((2, G, W), BF16),
            vmem((U, R, W), BF16),
            vmem((R, W), F32),
            vmem((8, 128), F32),
            vmem((T, 8, 128), F32),
            vmem((R, W), BF16),
            vmem((2, G, W), BF16),
            vmem((J, G, W), BF16),
            vmem((J, H, R, W), BF16),
            vmem((J, G, W), BF16),
            vmem((2, G, W), BF16),
            vmem((U, R, W), BF16),
            dma((6,)), dma((4,)), dma((4,)),
            dma((U,)), dma((2, H)), dma((B,)), dma((B,)), dma((T,)), dma((T,)), dma((U,)), dma((U,)),
            dma((H,)), dma((H,)), dma((3, H)), dma((3, H)), dma((B,)), dma((B,)), dma((2, 8)), dma((2, T)), dma((B,)), dma((B,)),
            dma((H,)), dma((H,)), dma((2, H)), dma((U,)), dma((T,)), dma((T,)), dma((U,)), dma((2, H)),
            dma((J, H)), dma((J, H)), dma((J, H)), dma((J, H)), dma((2, H)), dma((U,)),
        ],
        compiler_params=pltpu.CompilerParams(
            collective_id=0, has_side_effects=True, vmem_limit_bytes=48 * 1024 * 1024
        ),
        name="block_kernel",
    )(
        tokens,
        cond.reshape(1, -1),
        mod_weight.T,
        qkv_weight.transpose(1, 0, 2),
        q_gain.reshape(1, -1),
        k_gain.reshape(1, -1),
        out_weight,
        up_weight,
        down_weight,
    )


def solution(mesh):
    return jax.shard_map(
        on_device,
        mesh=mesh,
        in_specs=(
            P(("ulysses", "blk"), "tensor"),
            P(),
            P(None, ("ulysses", "blk", "tensor")),
            P("tensor", None, "ulysses"),
            P(),
            P(),
            P("ulysses", "tensor"),
            P("tensor", "ulysses"),
            P("ulysses", "tensor"),
        ),
        out_specs=P(("ulysses", "blk"), "tensor"),
        check_vma=False,
    )
```

```python
import functools
import math

import jax
import jax.numpy as jnp
from jax import lax
from jax.experimental import pallas as pl
from jax.experimental.pallas import tpu as pltpu
from jax.sharding import PartitionSpec as P

MESH = pl.DeviceIdType.MESH
F32 = jnp.float32
BF16 = jnp.bfloat16


def block_kernel(
    U, B, T,
    tokens, cond, mod_w, qkv_w, q_gain, k_gain, out_w, up_w, down_w,
    out,
    tok_own, cond_v, qg_v, kg_v, tok_rx, mw, wq, wo, wu, wd,
    m_tx, m_a, m_d, m_b, m_u, m_c, modv,
    st_tx, st_rx, rs_tx, rs_rb, rs_rx, q_rx, kv_rx, o_tx, o_rx, os_tx, os_rx, cf, cf_t, ctx_rx,
    at_tx, at_rx, mix, s2_tx, s2_rx, n2_tx, n2_rx, up_tx, up_rb, up_rx, act_rx, ff_tx, ff_rx,
    loc_sem, w_send, w_recv,
    tok_send, tok_recv, ma_send, ma_recv, mb_send, mb_recv, mc_send, mc_recv,
    st_send, st_recv, rs_send, rs_recv, q_send, q_recv, kv_send, kv_recv, km_send, km_recv, o_send, o_recv, os_send, os_recv,
    cx_send, cx_recv, at_send, at_recv, s2_send, s2_recv, n2_send, n2_recv,
    up_send, up_recv, ac_send, ac_recv, ff_send, ff_recv,
):
    C = 2
    H = T // C
    R, W = tokens.shape
    G = H * R
    features = W * T
    u = lax.axis_index("ulysses")
    b = lax.axis_index("blk")
    t = lax.axis_index("tensor")
    h = t // C
    c = lax.rem(t, C)
    mate = {"tensor": h * C + (1 - c)}
    uc = u // H
    ui = lax.rem(u, H)
    pending = []

    def rdma(src, dst, send, recv, dev):
        copy = pltpu.make_async_remote_copy(
            src_ref=src, dst_ref=dst, send_sem=send, recv_sem=recv,
            device_id=dev, device_id_type=MESH,
        )
        copy.start()
        pending.append((None, copy))

    def rdma_or_local(own, src, dst, send, recv, dev):
        copy = pltpu.make_async_remote_copy(
            src_ref=src, dst_ref=dst, send_sem=send, recv_sem=recv,
            device_id=dev, device_id_type=MESH,
        )

        @pl.when(own)
        def _():
            pltpu.make_async_copy(src, dst, recv).start()

        @pl.when(jnp.logical_not(own))
        def _():
            copy.start()

        pending.append((own, copy))

    def arrived(dst, recv):
        pltpu.make_async_copy(dst, dst, recv).wait()

    def y_peer(k):
        hp = lax.rem(h + k, H)
        return hp, {"tensor": hp * C + c}

    hr, right = y_peer(1)
    ho, _ = y_peer(2)
    hl, left = y_peer(3)
    R2 = R // 2

    def gather_start(rows, send, recv):
        mine = rows(h, 0, R)
        rdma(mine, mine, send(0), recv(0), right)
        rdma(mine, mine, send(1), recv(1), left)

    def gather_relay(rows, send, recv):
        arrived(rows(hl, 0, R), recv(0))
        part = rows(hl, 0, R2)
        rdma(part, part, send(2), recv(2), right)
        arrived(rows(hr, 0, R), recv(1))
        part = rows(hr, R2, R2)
        rdma(part, part, send(3), recv(3), left)

    def gather_end(rows, recv):
        arrived(rows(ho, 0, R2), recv(2))
        arrived(rows(ho, R2, R2), recv(3))

    def scatter_start(tx, rb, send, recv):
        rdma(tx.at[pl.ds(ho * R, R2), :], rb.at[0], send(0), recv(0), right)
        rdma(tx.at[pl.ds(ho * R + R2, R2), :], rb.at[1], send(1), recv(1), left)

    def scatter_relay(tx, rb, rx, send, recv):
        arrived(rb.at[0], recv(0))
        at = pl.ds(pl.multiple_of(hr * R, R2), R2)
        tx[at, :] = (tx[at, :].astype(F32) + rb[0].astype(F32)).astype(BF16)
        rdma(tx.at[pl.ds(hr * R, R), :], rx.at[0], send(2), recv(2), right)
        arrived(rb.at[1], recv(1))
        at = pl.ds(pl.multiple_of(hl * R + R2, R2), R2)
        tx[at, :] = (tx[at, :].astype(F32) + rb[1].astype(F32)).astype(BF16)
        rdma(tx.at[pl.ds(hl * R, R), :], rx.at[1], send(3), recv(3), left)

    def scatter_end(tx, rx, recv):
        arrived(rx.at[0], recv(2))
        arrived(rx.at[1], recv(3))
        own = tx[pl.ds(pl.multiple_of(h * R, R), R), :].astype(F32)
        return own + rx[0].astype(F32) + rx[1].astype(F32)

    barrier = pltpu.get_barrier_semaphore()
    count = 0
    for k in range(1, B):
        pl.semaphore_signal(barrier, inc=1, device_id={"blk": lax.rem(b + k, B)}, device_id_type=MESH)
        count += 1
    for k in range(1, T):
        pl.semaphore_signal(barrier, inc=1, device_id={"tensor": lax.rem(t + k, T)}, device_id_type=MESH)
        count += 1
    for k in range(1, U):
        for cc in range(C):
            pl.semaphore_signal(
                barrier, inc=1,
                device_id={"ulysses": lax.rem(u + k, U), "tensor": h * C + cc},
                device_id_type=MESH,
            )
            count += 1

    local = [
        pltpu.make_async_copy(mod_w, mw, loc_sem.at[0]),
        pltpu.make_async_copy(tokens, tok_own, loc_sem.at[1]),
        pltpu.make_async_copy(qkv_w, wq.at[:, c], loc_sem.at[2]),
        pltpu.make_async_copy(out_w, wo.at[c], loc_sem.at[3]),
        pltpu.make_async_copy(up_w, wu.at[c], loc_sem.at[4]),
        pltpu.make_async_copy(down_w, wd.at[c], loc_sem.at[5]),
        pltpu.make_async_copy(cond, cond_v, loc_sem.at[6]),
        pltpu.make_async_copy(q_gain, qg_v, loc_sem.at[7]),
        pltpu.make_async_copy(k_gain, kg_v, loc_sem.at[8]),
    ]
    for copy in local:
        copy.start()

    cf[...] = jnp.zeros_like(cf)
    local[6].wait()
    condf = cond_v[...].astype(F32)
    active = condf * jax.nn.sigmoid(condf)
    active = jnp.concatenate([active[i:i + 1] for i in range(features // 128)], axis=1).astype(BF16)
    local[0].wait()
    share = lax.dot_general(
        jnp.broadcast_to(active, (16, features)), mw[...],
        (((1,), (1,)), ((), ())), preferred_element_type=F32,
    )
    n_share = mod_w.shape[0]
    start = n_share * (b * T + t)
    lanes2 = lax.broadcasted_iota(jnp.int32, (n_share, 256), 1)
    rows2 = lax.broadcasted_iota(jnp.int32, (n_share, 256), 0)
    place = (lanes2 == rows2 + lax.rem(start, 128)).astype(F32)
    placed = jnp.dot(share[0:8], place, preferred_element_type=F32, precision=lax.Precision.HIGHEST)
    sub8 = lax.broadcasted_iota(jnp.int32, (8, 128), 0)
    tile = jnp.where(sub8 == 0, placed[:, 0:128], jnp.where(sub8 == 1, placed[:, 128:256], 0.0))
    m_tx[...] = tile
    m_a[b] = tile

    pl.semaphore_wait(barrier, count)

    for k in range(1, B):
        rdma(m_tx, m_a.at[b], ma_send.at[k], ma_recv.at[b], {"blk": lax.rem(b + k, B)})
    for up_ in range(U):
        rdma_or_local(
            jnp.logical_and(u == up_, c == uc),
            tokens, tok_rx.at[c, pl.ds(ui * R, R), :], tok_send.at[up_], tok_recv.at[c, ui],
            {"ulysses": up_, "tensor": h * C + uc},
        )
    rdma(qkv_w, wq.at[:, c], w_send.at[0], w_recv.at[0], mate)
    rdma(out_w, wo.at[c], w_send.at[1], w_recv.at[1], mate)
    rdma(up_w, wu.at[c], w_send.at[2], w_recv.at[2], mate)
    rdma(down_w, wd.at[c], w_send.at[3], w_recv.at[3], mate)

    per_u = n_share * B * T // 128
    m_d[...] = jnp.zeros_like(m_d)
    for k in range(B):
        if k:
            bp = lax.rem(b + k, B)
            arrived(m_a.at[bp], ma_recv.at[bp])
    for bp in range(B):
        row = (n_share * (bp * T + t)) // 128
        m_d[pl.ds(row, 1), :] += m_a[bp, 0:1, :]
        m_d[pl.ds(row + 1, 1), :] += m_a[bp, 1:2, :]
    m_b[t] = m_d[...]
    for k in range(1, T):
        rdma(m_d, m_b.at[t], mb_send.at[k], mb_recv.at[t], {"tensor": lax.rem(t + k, T)})

    for cc in range(C):
        for i in range(H):
            arrived(tok_rx.at[cc, pl.ds(i * R, R), :], tok_recv.at[cc, i])
    x0 = tok_rx[0].astype(F32)
    x1 = tok_rx[1].astype(F32)
    local_mean = (jnp.sum(x0, -1, keepdims=True) + jnp.sum(x1, -1, keepdims=True)) * (1.0 / (C * W))
    d0 = x0 - local_mean
    d1 = x1 - local_mean
    local_m2 = jnp.sum(d0 * d0, -1, keepdims=True) + jnp.sum(d1 * d1, -1, keepdims=True)
    lane = lax.broadcasted_iota(jnp.int32, (G, 128), 1)
    stats = jnp.where(lane == 0, local_mean, jnp.where(lane == 1, local_m2, 0.0))
    stats_t = jnp.transpose(stats)[0:8]
    st_tx[...] = stats_t
    st_rx[h] = stats_t
    for k in range(1, H):
        hp, dev = y_peer(k)
        rdma(st_tx, st_rx.at[h], st_send.at[k], st_recv.at[h], dev)

    for k in range(1, T):
        tp = lax.rem(t + k, T)
        arrived(m_b.at[tp], mb_recv.at[tp])
    dense = m_b[0]
    for tp in range(1, T):
        dense = dense + m_b[tp]
    m_u[...] = dense
    m_c[u] = dense
    for k in range(1, U):
        rdma(m_u, m_c.at[u], mc_send.at[k], mc_recv.at[u], {"ulysses": lax.rem(u + k, U)})

    for k in range(1, H):
        hp, _ = y_peer(k)
        arrived(st_rx.at[hp], st_recv.at[hp])
    mean = st_rx[0, 0:1, :]
    for hp in range(1, H):
        mean = mean + st_rx[hp, 0:1, :]
    mean = mean * (1.0 / H)
    m2 = jnp.zeros_like(mean)
    for hp in range(H):
        diff = st_rx[hp, 0:1, :] - mean
        m2 = m2 + st_rx[hp, 1:2, :] + (C * W) * diff * diff
    rstd = lax.rsqrt(m2 * (1.0 / features) + 1e-06)
    subg = lax.broadcasted_iota(jnp.int32, (128, G), 0)
    cols = jnp.transpose(jnp.where(subg == 0, mean, jnp.where(subg == 1, rstd, 0.0)))
    mean_c, rstd_c = cols[:, 0:1], cols[:, 1:2]

    for k in range(1, U):
        upk = lax.rem(u + k, U)
        arrived(m_c.at[upk], mc_recv.at[upk])
    for v in range(6):
        for k in range(C * W // 128):
            row = v * (features // 128) + h * (C * W // 128) + k
            modv[v:v + 1, 128 * k:128 * (k + 1)] = m_c[row // per_u, pl.ds(lax.rem(row, per_u), 1), :]

    n0 = ((x0 - mean_c) * rstd_c * (1.0 + modv[1:2, 0:W]) + modv[0:1, 0:W]).astype(BF16)
    n1 = ((x1 - mean_c) * rstd_c * (1.0 + modv[1:2, W:2 * W]) + modv[0:1, W:2 * W]).astype(BF16)

    local[2].wait()
    arrived(wq.at[:, 1 - c], w_recv.at[0])
    def rs_sems(sems, g):
        return lambda k: sems.at[g, k]

    for g in range(3):
        part = jnp.dot(n0, wq[g, 0], preferred_element_type=F32)
        part = part + jnp.dot(n1, wq[g, 1], preferred_element_type=F32)
        rs_tx[g] = part.astype(BF16)
        scatter_start(rs_tx.at[g], rs_rb.at[g], rs_sems(rs_send, g), rs_sems(rs_recv, g))

    heads = W // 128

    def proj_relay(g):
        scatter_relay(rs_tx.at[g], rs_rb.at[g], rs_rx.at[g], rs_sems(rs_send, g), rs_sems(rs_recv, g))

    def kv_rows(g):
        return lambda hp, lo, n: kv_rx.at[g, pl.ds((c * H + hp) * R + lo, n), :]

    def to_mate(g, hp, i):
        rows = kv_rows(g)(hp, 0, R)
        rdma(rows, rows, km_send.at[g, i], km_recv.at[g, hp], mate)

    def proj_end(g):
        total = scatter_end(rs_tx.at[g], rs_rx.at[g], rs_sems(rs_recv, g))
        if g < 2:
            local[7 + g].wait()
            gain = (qg_v if g == 0 else kg_v)[...]
            pieces = []
            for hd in range(heads):
                piece = total[:, 128 * hd:128 * (hd + 1)]
                ms = jnp.mean(piece * piece, axis=-1, keepdims=True)
                pieces.append(piece * lax.rsqrt(ms + 1e-06) * gain)
            total = jnp.concatenate(pieces, axis=1)
        if g == 0:
            rows = q_rx.at[pl.ds(b * R, R), :]
            q_rx[pl.ds(pl.multiple_of(b * R, R), R), :] = total.astype(BF16)
            for k in sorted(range(1, B), key=lambda k: -min(k, B - k)):
                rdma(rows, rows, q_send.at[k], q_recv.at[b], {"blk": lax.rem(b + k, B)})
        else:
            kv_rx[g - 1, pl.ds(pl.multiple_of((c * H + h) * R, R), R), :] = total.astype(BF16)
            gather_start(kv_rows(g - 1), rs_sems(kv_send, g - 1), rs_sems(kv_recv, g - 1))
            to_mate(g - 1, h, 0)

    proj_relay(0)
    proj_relay(1)
    proj_end(0)
    proj_relay(2)
    proj_end(1)
    proj_end(2)
    for g in range(2):
        gather_relay(kv_rows(g), rs_sems(kv_send, g), rs_sems(kv_recv, g))
        to_mate(g, hl, 1)
        to_mate(g, hr, 2)
    for g in range(2):
        gather_end(kv_rows(g), rs_sems(kv_recv, g))
        to_mate(g, ho, 3)
    for k in range(1, B):
        bp = lax.rem(b + k, B)
        arrived(q_rx.at[pl.ds(bp * R, R), :], q_recv.at[bp])
    for g in range(2):
        for hp in range(H):
            arrived(kv_rx.at[g, pl.ds(((1 - c) * H + hp) * R, R), :], km_recv.at[g, hp])

    scale = 1.0 / math.sqrt(128)
    QB = 2 * R
    nq = B // 2
    rest = []
    for i, off in enumerate(sorted(range(nq), key=lambda k: -min(k, nq - k))):
        qb = lax.rem(b // 2 + off, nq)
        at = pl.multiple_of(qb * QB, QB)
        lane_q = lax.broadcasted_iota(jnp.int32, (QB, 128), 1)
        tail = jnp.zeros((QB, 128), F32)
        for hd in range(heads):
            cut = slice(128 * hd, 128 * (hd + 1))
            s = lax.dot_general(
                q_rx[pl.ds(at, QB), cut], kv_rx[0, :, cut],
                (((1,), (1,)), ((), ())), preferred_element_type=F32,
            )
            top = jnp.max(s, axis=-1, keepdims=True)
            p = jnp.exp((s - top) * scale)
            weight = jnp.sum(p, axis=-1, keepdims=True)
            o = jnp.dot(p.astype(BF16), kv_rx[1, :, cut], preferred_element_type=F32)
            o_tx[pl.ds(at, QB), cut] = o.astype(BF16)
            tail = jnp.where(lane_q == hd, top, tail)
            tail = jnp.where(lane_q == heads + hd, weight, tail)
        os_tx[qb] = jnp.transpose(tail)[0:8]
        targets = [2 * qb, 2 * qb + 1]
        if off == 0:
            o_rx[b] = o_tx[pl.ds(pl.multiple_of(b * R, R), R), :]
            os_rx[b] = os_tx[qb]
            targets = [b + 1 - 2 * lax.rem(b, 2)]
        for e, bp in enumerate(targets):
            dev = {"blk": bp}
            rdma(o_tx.at[pl.ds(bp * R, R), :], o_rx.at[b], o_send.at[2 * i + e], o_recv.at[b], dev)
            rdma(os_tx.at[qb], os_rx.at[b], os_send.at[2 * i + e], os_recv.at[b], dev)
    for k in range(1, B):
        bp = lax.rem(b + k, B)
        arrived(os_rx.at[bp], os_recv.at[bp])
    for hd in range(heads):
        tops = [os_rx[bp, hd:hd + 1, :] for bp in range(B)]
        top = functools.reduce(jnp.maximum, tops)
        shares = [jnp.exp((tops[bp] - top) * scale) for bp in range(B)]
        den = shares[0] * os_rx[0, heads + hd:heads + hd + 1, :]
        for bp in range(1, B):
            den = den + shares[bp] * os_rx[bp, heads + hd:heads + hd + 1, :]
        for bp in range(B):
            cf[hd * B + bp:hd * B + bp + 1, :] = shares[bp] / den
    cf_t[...] = jnp.transpose(cf[...])
    coef = cf_t[pl.ds(pl.multiple_of(lax.rem(b, 2) * R, R), R), :]
    for k in range(1, B):
        bp = lax.rem(b + k, B)
        arrived(o_rx.at[bp], o_recv.at[bp])
    pieces = []
    for hd in range(heads):
        cut = slice(128 * hd, 128 * (hd + 1))
        num = coef[:, hd * B:hd * B + 1] * o_rx[0, :, cut].astype(F32)
        for bp in range(1, B):
            num = num + coef[:, hd * B + bp:hd * B + bp + 1] * o_rx[bp, :, cut].astype(F32)
        pieces.append(num)

    def ctx_rows(hp, lo, n):
        return ctx_rx.at[pl.ds(hp * R + lo, n), :]

    ctx_rx[pl.ds(pl.multiple_of(h * R, R), R), :] = jnp.concatenate(pieces, axis=1).astype(BF16)
    gather_start(ctx_rows, lambda k: cx_send.at[k], lambda k: cx_recv.at[k])
    gather_relay(ctx_rows, lambda k: cx_send.at[k], lambda k: cx_recv.at[k])
    local[3].wait()
    arrived(wo.at[1 - c], w_recv.at[1])
    gather_end(ctx_rows, lambda k: cx_recv.at[k])

    def to_owners(tx, rx, send, recv, cc):
        for hp in range(H):
            up_ = c * H + hp
            rdma_or_local(
                jnp.logical_and(up_ == u, c == cc),
                tx.at[cc, pl.ds(hp * R, R), :], rx.at[u], send.at[cc, hp], recv.at[u],
                {"ulysses": up_, "tensor": h * C + cc},
            )

    for cc in range(C):
        at_tx[cc] = jnp.dot(ctx_rx[...], wo[cc], preferred_element_type=F32).astype(BF16)
        to_owners(at_tx, at_rx, at_send, at_recv, cc)
    for up_ in range(U):
        arrived(at_rx.at[up_], at_recv.at[up_])
    attended = at_rx[0].astype(F32)
    for up_ in range(1, U):
        attended = attended + at_rx[up_].astype(F32)
    local[1].wait()
    own_cols = pl.ds(pl.multiple_of(c * W, 128), W)
    mixed = tok_own[...].astype(F32) + modv[2:3, own_cols] * attended
    mix[...] = mixed

    mean_l = jnp.sum(mixed, -1, keepdims=True) * (1.0 / W)
    diff = mixed - mean_l
    m2_l = jnp.sum(diff * diff, -1, keepdims=True)
    lane_r = lax.broadcasted_iota(jnp.int32, (R, 128), 1)
    st2 = jnp.where(lane_r == 0, mean_l, jnp.where(lane_r == 1, m2_l, 0.0))
    st2_t = jnp.transpose(jnp.concatenate([st2, jnp.zeros((128 - R, 128), F32)], axis=0))[0:8]
    s2_tx[...] = st2_t
    s2_rx[t] = st2_t
    for k in range(1, T):
        rdma(s2_tx, s2_rx.at[t], s2_send.at[k], s2_recv.at[t], {"tensor": lax.rem(t + k, T)})
    for k in range(1, T):
        tp = lax.rem(t + k, T)
        arrived(s2_rx.at[tp], s2_recv.at[tp])
    total = s2_rx[0]
    for tp in range(1, T):
        total = total + s2_rx[tp]
    mean2 = total[0:1] * (1.0 / T)
    m2 = total[1:2]
    for tp in range(T):
        dev2 = s2_rx[tp, 0:1, :] - mean2
        m2 = m2 + W * dev2 * dev2
    rstd2 = lax.rsqrt(m2 * (1.0 / features) + 1e-06)
    sub2 = lax.broadcasted_iota(jnp.int32, (128, 128), 0)
    cols2 = jnp.transpose(jnp.where(sub2 == 0, mean2, jnp.where(sub2 == 1, rstd2, 0.0)))
    normed = (mixed - cols2[0:R, 0:1]) * cols2[0:R, 1:2]
    n2_tx[...] = (normed * (1.0 + modv[4:5, own_cols]) + modv[3:4, own_cols]).astype(BF16)
    for up_ in range(U):
        rdma_or_local(
            jnp.logical_and(u == up_, c == uc),
            n2_tx, n2_rx.at[c, pl.ds(ui * R, R), :], n2_send.at[up_], n2_recv.at[c, ui],
            {"ulysses": up_, "tensor": h * C + uc},
        )
    local[4].wait()
    arrived(wu.at[1 - c], w_recv.at[2])
    for cc in range(C):
        for i in range(H):
            arrived(n2_rx.at[cc, pl.ds(i * R, R), :], n2_recv.at[cc, i])

    J = up_w.shape[1] // W

    def act_rows(j):
        return lambda hp, lo, n: act_rx.at[j, pl.ds(hp * R + lo, n), :]

    for j in range(J):
        cut = slice(W * j, W * (j + 1))
        part = jnp.dot(n2_rx[0], wu[0, :, cut], preferred_element_type=F32)
        part = part + jnp.dot(n2_rx[1], wu[1, :, cut], preferred_element_type=F32)
        up_tx[j] = part.astype(BF16)
        scatter_start(up_tx.at[j], up_rb.at[j], rs_sems(up_send, j), rs_sems(up_recv, j))

    def ff_relay(j):
        scatter_relay(up_tx.at[j], up_rb.at[j], up_rx.at[j], rs_sems(up_send, j), rs_sems(up_recv, j))

    def ff_end(j):
        hidden = scatter_end(up_tx.at[j], up_rx.at[j], rs_sems(up_recv, j))
        act_rx[j, pl.ds(pl.multiple_of(h * R, R), R), :] = jax.nn.gelu(hidden, approximate=True).astype(BF16)
        gather_start(act_rows(j), rs_sems(ac_send, j), rs_sems(ac_recv, j))

    def act_relay(j):
        gather_relay(act_rows(j), rs_sems(ac_send, j), rs_sems(ac_recv, j))

    accs = [None] * C

    def act_end(j):
        gather_end(act_rows(j), rs_sems(ac_recv, j))
        for cc in range(C):
            part = jnp.dot(act_rx[j], wd[cc, W * j:W * (j + 1), :], preferred_element_type=F32)
            accs[cc] = part if j == 0 else accs[cc] + part

    steps = []
    for j in range(J):
        for n, step in enumerate((ff_relay, ff_end, act_relay, act_end)):
            steps.append((j + 1.5 * n, n, j, step))
    waited = False
    for _, n, j, step in sorted(steps, key=lambda item: item[:3]):
        if n == 3 and not waited:
            local[5].wait()
            arrived(wd.at[1 - c], w_recv.at[3])
            waited = True
        step(j)
    for cc in range(C):
        ff_tx[cc] = accs[cc].astype(BF16)
        to_owners(ff_tx, ff_rx, ff_send, ff_recv, cc)
    for up_ in range(U):
        arrived(ff_rx.at[up_], ff_recv.at[up_])
    feed = ff_rx[0].astype(F32)
    for up_ in range(1, U):
        feed = feed + ff_rx[up_].astype(F32)
    out[...] = mix[...] + modv[5:6, own_cols] * feed

    for own, copy in pending:
        if own is None:
            copy.wait_send()
        else:
            pl.when(jnp.logical_not(own))(copy.wait_send)


def on_device(
    tokens, cond, mod_weight, qkv_weight, q_gain, k_gain, out_weight, up_weight, down_weight
):
    U = lax.axis_size("ulysses")
    B = lax.axis_size("blk")
    T = lax.axis_size("tensor")
    H = T // 2
    R, W = tokens.shape
    G = H * R
    FFL = up_weight.shape[1]
    J = FFL // W
    dma = pltpu.SemaphoreType.DMA
    vmem = pltpu.VMEM
    any_spec = pl.BlockSpec(memory_space=pltpu.HBM)
    vm_spec = pl.BlockSpec(memory_space=pltpu.VMEM)
    return pl.pallas_call(
        functools.partial(block_kernel, U, B, T),
        out_shape=jax.ShapeDtypeStruct((R, W), F32),
        in_specs=[any_spec] * 9,
        out_specs=vm_spec,
        scratch_shapes=[
            vmem((R, W), BF16),
            vmem((mod_weight.shape[0] // 128, 128), BF16),
            vmem((1, 128), F32),
            vmem((1, 128), F32),
            vmem((2, G, W), BF16),
            vmem((mod_weight.shape[1], mod_weight.shape[0]), BF16),
            vmem((3, 2, W, W), BF16),
            vmem((2, W, W), BF16),
            vmem((2, W, FFL), BF16),
            vmem((2, FFL, W), BF16),
            vmem((8, 128), F32),
            vmem((B, 8, 128), F32),
            vmem((24, 128), F32),
            vmem((T, 24, 128), F32),
            vmem((24, 128), F32),
            vmem((U, 24, 128), F32),
            vmem((8, 2 * W), F32),
            vmem((8, G), F32),
            vmem((H, 8, G), F32),
            vmem((3, G, W), BF16),
            vmem((3, 2, R // 2, W), BF16),
            vmem((3, 2, R, W), BF16),
            vmem((B * R, W), BF16),
            vmem((2, T * R, W), BF16),
            vmem((B * R, W), BF16),
            vmem((B, R, W), BF16),
            vmem((B // 2, 8, 128), F32),
            vmem((B, 8, 128), F32),
            vmem((128, 128), F32),
            vmem((128, 128), F32),
            vmem((G, W), BF16),
            vmem((2, G, W), BF16),
            vmem((U, R, W), BF16),
            vmem((R, W), F32),
            vmem((8, 128), F32),
            vmem((T, 8, 128), F32),
            vmem((R, W), BF16),
            vmem((2, G, W), BF16),
            vmem((J, G, W), BF16),
            vmem((J, 2, R // 2, W), BF16),
            vmem((J, 2, R, W), BF16),
            vmem((J, G, W), BF16),
            vmem((2, G, W), BF16),
            vmem((U, R, W), BF16),
            dma((9,)), dma((4,)), dma((4,)),
            dma((U,)), dma((2, H)), dma((B,)), dma((B,)), dma((T,)), dma((T,)), dma((U,)), dma((U,)),
            dma((H,)), dma((H,)), dma((3, H)), dma((3, H)), dma((B,)), dma((B,)), dma((2, H)), dma((2, H)), dma((2, H)), dma((2, H)), dma((B,)), dma((B,)), dma((B,)), dma((B,)),
            dma((H,)), dma((H,)), dma((2, H)), dma((U,)), dma((T,)), dma((T,)), dma((U,)), dma((2, H)),
            dma((J, H)), dma((J, H)), dma((J, H)), dma((J, H)), dma((2, H)), dma((U,)),
        ],
        compiler_params=pltpu.CompilerParams(
            collective_id=0, has_side_effects=True, vmem_limit_bytes=67043328
        ),
        name="block_kernel",
    )(
        tokens,
        cond.reshape(-1, 128),
        mod_weight.T,
        qkv_weight.transpose(1, 0, 2),
        q_gain.reshape(1, -1),
        k_gain.reshape(1, -1),
        out_weight,
        up_weight,
        down_weight,
    )


def solution(mesh):
    return jax.shard_map(
        on_device,
        mesh=mesh,
        in_specs=(
            P(("ulysses", "blk"), "tensor"),
            P(),
            P(None, ("ulysses", "blk", "tensor")),
            P("tensor", None, "ulysses"),
            P(),
            P(),
            P("ulysses", "tensor"),
            P("tensor", "ulysses"),
            P("ulysses", "tensor"),
        ),
        out_specs=P(("ulysses", "blk"), "tensor"),
        check_vma=False,
    )
```

```python
import functools
import math

import jax
import jax.numpy as jnp
from jax import lax
from jax.experimental import pallas as pl
from jax.experimental.pallas import tpu as pltpu
from jax.sharding import PartitionSpec as P

ORDER = [int(s) for s in "01001010101001010011010101011101"]
MESH = pl.DeviceIdType.MESH
F32 = jnp.float32
BF16 = jnp.bfloat16


def block_kernel(
    U, B, T,
    tokens, cond, mod_w, qkv_w, q_gain, k_gain, out_w, up_w, down_w,
    out,
    tok_own, cond_v, qg_v, kg_v, tok_rx, mw, wq, wo, wu, wd,
    m_tx, m_a, m_d, m_b, m_u, m_c, modv,
    st_tx, st_rx, rs_tx, rs_rb, rs_rx, q_rx, kv_rx, o_tx, o_rx, os_tx, os_rx, cf, cf_t, ctx_rx,
    at_tx, at_rx, mix, s2_tx, s2_rx, fx_tx, fx_rx, cv_tx, cv_rx, n2_tx, n2_rx, up_tx, up_rb, up_rx, act_rx, ff_tx, ff_rx,
    loc_sem, w_send, w_recv,
    tok_send, tok_recv, ma_send, ma_recv, mb_send, mb_recv, mc_send, mc_recv,
    st_send, st_recv, rs_send, rs_recv, q_send, q_recv, kv_send, kv_recv, km_send, km_recv, o_send, o_recv, os_send, os_recv,
    cx_send, cx_recv, at_send, at_recv, s2_send, s2_recv, fx_send, fx_recv, cv_send, cv_recv, n2_send, n2_recv,
    up_send, up_recv, ac_send, ac_recv, ff_send, ff_recv,
):
    C = 2
    H = T // C
    R, W = tokens.shape
    G = H * R
    S = 2
    N = R // S
    GN = H * N
    features = W * T
    u = lax.axis_index("ulysses")
    b = lax.axis_index("blk")
    t = lax.axis_index("tensor")
    h = t // C
    c = lax.rem(t, C)
    mate = {"tensor": h * C + (1 - c)}
    uc = u // H
    ui = lax.rem(u, H)
    pending = []

    def rdma(src, dst, send, recv, dev):
        copy = pltpu.make_async_remote_copy(
            src_ref=src, dst_ref=dst, send_sem=send, recv_sem=recv,
            device_id=dev, device_id_type=MESH,
        )
        copy.start()
        pending.append((None, copy))

    def rdma_or_local(own, src, dst, send, recv, dev):
        copy = pltpu.make_async_remote_copy(
            src_ref=src, dst_ref=dst, send_sem=send, recv_sem=recv,
            device_id=dev, device_id_type=MESH,
        )

        @pl.when(own)
        def _():
            pltpu.make_async_copy(src, dst, recv).start()

        @pl.when(jnp.logical_not(own))
        def _():
            copy.start()

        pending.append((own, copy))

    def arrived(dst, recv):
        pltpu.make_async_copy(dst, dst, recv).wait()

    def y_peer(k):
        hp = lax.rem(h + k, H)
        return hp, {"tensor": hp * C + c}

    hr, right = y_peer(1)
    ho, _ = y_peer(2)
    hl, left = y_peer(3)

    def gather_start(rows, n, send, recv):
        mine = rows(h, 0, n)
        rdma(mine, mine, send(0), recv(0), right)
        rdma(mine, mine, send(1), recv(1), left)

    def gather_relay(rows, n, send, recv):
        half = n // 2
        arrived(rows(hl, 0, n), recv(0))
        part = rows(hl, 0, half)
        rdma(part, part, send(2), recv(2), right)
        arrived(rows(hr, 0, n), recv(1))
        part = rows(hr, half, half)
        rdma(part, part, send(3), recv(3), left)

    def gather_end(rows, n, recv):
        half = n // 2
        arrived(rows(ho, 0, half), recv(2))
        arrived(rows(ho, half, half), recv(3))

    def scatter_start(tx, rb, n, send, recv):
        half = n // 2
        rdma(tx.at[pl.ds(ho * n, half), :], rb.at[0], send(0), recv(0), right)
        rdma(tx.at[pl.ds(ho * n + half, half), :], rb.at[1], send(1), recv(1), left)

    def scatter_relay(tx, rb, rx, n, send, recv):
        half = n // 2
        for side, (to, dev) in enumerate(((hr, right), (hl, left))):
            arrived(rb.at[side], recv(side))
            at = pl.ds(pl.multiple_of(to * n + side * half, half), half)
            tx[at, :] = (tx[at, :].astype(F32) + rb[side].astype(F32)).astype(BF16)
            rdma(tx.at[pl.ds(to * n, n), :], rx.at[side], send(2 + side), recv(2 + side), dev)

    def scatter_end(tx, rx, n, recv):
        arrived(rx.at[0], recv(2))
        arrived(rx.at[1], recv(3))
        own = tx[pl.ds(pl.multiple_of(h * n, n), n), :].astype(F32)
        return own + rx[0].astype(F32) + rx[1].astype(F32)

    barrier = pltpu.get_barrier_semaphore()
    count = 0
    for k in range(1, B):
        pl.semaphore_signal(barrier, inc=1, device_id={"blk": lax.rem(b + k, B)}, device_id_type=MESH)
        count += 1
    for k in range(1, T):
        pl.semaphore_signal(barrier, inc=1, device_id={"tensor": lax.rem(t + k, T)}, device_id_type=MESH)
        count += 1
    for k in range(1, U):
        for cc in range(C):
            pl.semaphore_signal(
                barrier, inc=1,
                device_id={"ulysses": lax.rem(u + k, U), "tensor": h * C + cc},
                device_id_type=MESH,
            )
            count += 1

    local = [
        pltpu.make_async_copy(mod_w, mw, loc_sem.at[0]),
        pltpu.make_async_copy(tokens, tok_own, loc_sem.at[1]),
        pltpu.make_async_copy(qkv_w, wq.at[:, c], loc_sem.at[2]),
        pltpu.make_async_copy(out_w, wo.at[c], loc_sem.at[3]),
        pltpu.make_async_copy(up_w, wu.at[c], loc_sem.at[4]),
        pltpu.make_async_copy(down_w, wd.at[c], loc_sem.at[5]),
        pltpu.make_async_copy(cond, cond_v, loc_sem.at[6]),
        pltpu.make_async_copy(q_gain, qg_v, loc_sem.at[7]),
        pltpu.make_async_copy(k_gain, kg_v, loc_sem.at[8]),
    ]
    for copy in local:
        copy.start()

    cf[...] = jnp.zeros_like(cf)
    local[6].wait()
    condf = cond_v[...].astype(F32)
    active = condf * jax.nn.sigmoid(condf)
    active = jnp.concatenate([active[i:i + 1] for i in range(features // 128)], axis=1).astype(BF16)
    local[0].wait()
    share = lax.dot_general(
        jnp.broadcast_to(active, (16, features)), mw[...],
        (((1,), (1,)), ((), ())), preferred_element_type=F32,
    )
    n_share = mod_w.shape[0]
    start = n_share * (b * T + t)
    lanes2 = lax.broadcasted_iota(jnp.int32, (n_share, 256), 1)
    rows2 = lax.broadcasted_iota(jnp.int32, (n_share, 256), 0)
    place = (lanes2 == rows2 + lax.rem(start, 128)).astype(F32)
    placed = jnp.dot(share[0:8], place, preferred_element_type=F32, precision=lax.Precision.HIGHEST)
    sub8 = lax.broadcasted_iota(jnp.int32, (8, 128), 0)
    tile = jnp.where(sub8 == 0, placed[:, 0:128], jnp.where(sub8 == 1, placed[:, 128:256], 0.0))
    m_tx[...] = tile
    m_a[b] = tile

    pl.semaphore_wait(barrier, count)

    for k in range(1, B):
        rdma(m_tx, m_a.at[b], ma_send.at[k], ma_recv.at[b], {"blk": lax.rem(b + k, B)})
    for up_ in range(U):
        rdma_or_local(
            jnp.logical_and(u == up_, c == uc),
            tokens, tok_rx.at[c, pl.ds(ui * R, R), :], tok_send.at[up_], tok_recv.at[c, ui],
            {"ulysses": up_, "tensor": h * C + uc},
        )
    rdma(qkv_w, wq.at[:, c], w_send.at[0], w_recv.at[0], mate)
    rdma(out_w, wo.at[c], w_send.at[1], w_recv.at[1], mate)
    rdma(up_w, wu.at[c], w_send.at[2], w_recv.at[2], mate)
    rdma(down_w, wd.at[c], w_send.at[3], w_recv.at[3], mate)

    per_u = n_share * B * T // 128
    m_d[...] = jnp.zeros_like(m_d)
    for k in range(B):
        if k:
            bp = lax.rem(b + k, B)
            arrived(m_a.at[bp], ma_recv.at[bp])
    for bp in range(B):
        row = (n_share * (bp * T + t)) // 128
        m_d[pl.ds(row, 1), :] += m_a[bp, 0:1, :]
        m_d[pl.ds(row + 1, 1), :] += m_a[bp, 1:2, :]
    m_b[t] = m_d[...]
    for k in range(1, T):
        rdma(m_d, m_b.at[t], mb_send.at[k], mb_recv.at[t], {"tensor": lax.rem(t + k, T)})

    for cc in range(C):
        for i in range(H):
            arrived(tok_rx.at[cc, pl.ds(i * R, R), :], tok_recv.at[cc, i])
    x0 = tok_rx[0].astype(F32)
    x1 = tok_rx[1].astype(F32)
    local_mean = (jnp.sum(x0, -1, keepdims=True) + jnp.sum(x1, -1, keepdims=True)) * (1.0 / (C * W))
    d0 = x0 - local_mean
    d1 = x1 - local_mean
    local_m2 = jnp.sum(d0 * d0, -1, keepdims=True) + jnp.sum(d1 * d1, -1, keepdims=True)
    lane = lax.broadcasted_iota(jnp.int32, (G, 128), 1)
    stats = jnp.where(lane == 0, local_mean, jnp.where(lane == 1, local_m2, 0.0))
    stats_t = jnp.transpose(stats)[0:8]
    st_tx[...] = stats_t
    st_rx[h] = stats_t
    for k in range(1, H):
        hp, dev = y_peer(k)
        rdma(st_tx, st_rx.at[h], st_send.at[k], st_recv.at[h], dev)

    for k in range(1, T):
        tp = lax.rem(t + k, T)
        arrived(m_b.at[tp], mb_recv.at[tp])
    dense = m_b[0]
    for tp in range(1, T):
        dense = dense + m_b[tp]
    m_u[...] = dense
    m_c[u] = dense
    for k in range(1, U):
        rdma(m_u, m_c.at[u], mc_send.at[k], mc_recv.at[u], {"ulysses": lax.rem(u + k, U)})

    for k in range(1, H):
        hp, _ = y_peer(k)
        arrived(st_rx.at[hp], st_recv.at[hp])
    mean = st_rx[0, 0:1, :]
    for hp in range(1, H):
        mean = mean + st_rx[hp, 0:1, :]
    mean = mean * (1.0 / H)
    m2 = jnp.zeros_like(mean)
    for hp in range(H):
        diff = st_rx[hp, 0:1, :] - mean
        m2 = m2 + st_rx[hp, 1:2, :] + (C * W) * diff * diff
    rstd = lax.rsqrt(m2 * (1.0 / features) + 1e-06)
    subg = lax.broadcasted_iota(jnp.int32, (128, G), 0)
    cols = jnp.transpose(jnp.where(subg == 0, mean, jnp.where(subg == 1, rstd, 0.0)))
    mean_c, rstd_c = cols[:, 0:1], cols[:, 1:2]

    for k in range(1, U):
        upk = lax.rem(u + k, U)
        arrived(m_c.at[upk], mc_recv.at[upk])
    for v in range(6):
        for k in range(C * W // 128):
            row = v * (features // 128) + h * (C * W // 128) + k
            modv[v:v + 1, 128 * k:128 * (k + 1)] = m_c[row // per_u, pl.ds(lax.rem(row, per_u), 1), :]

    n0 = ((x0 - mean_c) * rstd_c * (1.0 + modv[1:2, 0:W]) + modv[0:1, 0:W]).astype(BF16)
    n1 = ((x1 - mean_c) * rstd_c * (1.0 + modv[1:2, W:2 * W]) + modv[0:1, W:2 * W]).astype(BF16)

    local[2].wait()
    arrived(wq.at[:, 1 - c], w_recv.at[0])
    def rs_sems(sems, g):
        return lambda k: sems.at[g, k]

    for g in range(3):
        part = jnp.dot(n0, wq[g, 0], preferred_element_type=F32)
        part = part + jnp.dot(n1, wq[g, 1], preferred_element_type=F32)
        rs_tx[g] = part.astype(BF16)
        scatter_start(rs_tx.at[g], rs_rb.at[g], R, rs_sems(rs_send, g), rs_sems(rs_recv, g))

    heads = W // 128

    def proj_relay(g):
        scatter_relay(rs_tx.at[g], rs_rb.at[g], rs_rx.at[g], R, rs_sems(rs_send, g), rs_sems(rs_recv, g))

    def kv_rows(g):
        return lambda hp, lo, n: kv_rx.at[g, pl.ds((c * H + hp) * R + lo, n), :]

    def to_mate(g, hp, i):
        rows = kv_rows(g)(hp, 0, R)
        rdma(rows, rows, km_send.at[g, i], km_recv.at[g, hp], mate)

    def proj_end(g):
        total = scatter_end(rs_tx.at[g], rs_rx.at[g], R, rs_sems(rs_recv, g))
        if g < 2:
            local[7 + g].wait()
            gain = (qg_v if g == 0 else kg_v)[...]
            pieces = []
            for hd in range(heads):
                piece = total[:, 128 * hd:128 * (hd + 1)]
                ms = jnp.mean(piece * piece, axis=-1, keepdims=True)
                pieces.append(piece * lax.rsqrt(ms + 1e-06) * gain)
            total = jnp.concatenate(pieces, axis=1)
        if g == 0:
            for s in range(S):
                q_rx[s, pl.ds(pl.multiple_of(b * N, N), N), :] = total[s * N:(s + 1) * N].astype(BF16)
                rows = q_rx.at[s, pl.ds(b * N, N), :]
                for k in sorted(range(1, B), key=lambda k: -min(k, B - k)):
                    rdma(rows, rows, q_send.at[s, k], q_recv.at[s, b], {"blk": lax.rem(b + k, B)})
        else:
            kv_rx[g - 1, pl.ds(pl.multiple_of((c * H + h) * R, R), R), :] = total.astype(BF16)
            gather_start(kv_rows(g - 1), R, rs_sems(kv_send, g - 1), rs_sems(kv_recv, g - 1))
            to_mate(g - 1, h, 0)

    local[4].wait()
    arrived(wu.at[1 - c], w_recv.at[2])
    for cc in range(C):
        cut = slice(cc * W, (cc + 1) * W)
        vecs = []
        for vec in (1.0 + modv[4:5, cut], modv[3:4, cut]):
            high = vec.astype(BF16).astype(F32)
            vecs += [high, vec - high]
        sub16 = lax.broadcasted_iota(jnp.int32, (16, W), 0)
        left_side = jnp.zeros((16, W), F32)
        for i, vec in enumerate(vecs):
            left_side = jnp.where(sub16 == i, vec, left_side)
        cols16 = jnp.dot(left_side.astype(BF16), wu[cc], preferred_element_type=F32)
        cv_tx[cc:cc + 1, :] = cols16[0:1] + cols16[1:2]
        shifted = cols16[2:3] + cols16[3:4]
        cv_tx[2:3, :] = shifted if cc == 0 else cv_tx[2:3, :] + shifted
    cv_tx[3:8, :] = jnp.zeros((5, wu.shape[2]), F32)
    cv_rx[h] = cv_tx[...]

    proj_relay(0)
    proj_relay(1)
    proj_end(0)
    proj_relay(2)
    proj_end(1)
    proj_end(2)
    for g in range(2):
        gather_relay(kv_rows(g), R, rs_sems(kv_send, g), rs_sems(kv_recv, g))
        to_mate(g, hl, 1)
        to_mate(g, hr, 2)
    for g in range(2):
        gather_end(kv_rows(g), R, rs_sems(kv_recv, g))
        to_mate(g, ho, 3)
    for k in range(1, B):
        bp = lax.rem(b + k, B)
        for s in range(S):
            arrived(q_rx.at[s, pl.ds(bp * N, N), :], q_recv.at[s, bp])
    for g in range(2):
        for hp in range(H):
            arrived(kv_rx.at[g, pl.ds(((1 - c) * H + hp) * R, R), :], km_recv.at[g, hp])

    scale = 1.0 / math.sqrt(128)
    TB = 128 // N
    nq = B // TB
    own_cols = pl.ds(pl.multiple_of(c * W, 128), W)
    J, FW = up_tx.shape[1], up_tx.shape[3]

    def sems(ref, *index):
        return lambda k: ref.at[(*index, k)]

    def to_owners(s, tx, rx, send, recv, cc):
        for hp in range(H):
            up_ = c * H + hp
            rdma_or_local(
                jnp.logical_and(up_ == u, c == cc),
                tx.at[s, cc, pl.ds(hp * N, N), :], rx.at[s, u], send.at[s, cc, hp], recv.at[s, u],
                {"ulysses": up_, "tensor": h * C + cc},
            )

    def from_owners(s, rx, recv):
        for up_ in range(U):
            arrived(rx.at[s, up_], recv.at[s, up_])
        total = rx[s, 0].astype(F32)
        for up_ in range(1, U):
            total = total + rx[s, up_].astype(F32)
        return total

    def fix_copies(s):
        return [
            pltpu.make_async_remote_copy(
                src_ref=fx_tx.at[s], dst_ref=fx_rx.at[s], send_sem=fx_send.at[s, k], recv_sem=fx_recv.at[s],
                device_id={"ulysses": lax.rem(u + k, U)}, device_id_type=MESH,
            )
            for k in range(1, U)
        ]

    def part_steps(s):
        for off in range(nq - 1, -1, -1):
            qb = lax.rem(b // TB + off, nq)
            at = pl.multiple_of(qb * 128, 128)
            lane_q = lax.broadcasted_iota(jnp.int32, (128, 128), 1)
            tail = jnp.zeros((128, 128), F32)
            for hd in range(heads):
                cut = slice(128 * hd, 128 * (hd + 1))
                score = lax.dot_general(
                    q_rx[s, pl.ds(at, 128), cut], kv_rx[0, :, cut],
                    (((1,), (1,)), ((), ())), preferred_element_type=F32,
                )
                top = jnp.max(score, axis=-1, keepdims=True)
                p = jnp.exp((score - top) * scale)
                weight = jnp.sum(p, axis=-1, keepdims=True)
                o = jnp.dot(p.astype(BF16), kv_rx[1, :, cut], preferred_element_type=F32)
                o_tx[s, pl.ds(at, 128), cut] = o.astype(BF16)
                tail = jnp.where(lane_q == hd, top, tail)
                tail = jnp.where(lane_q == heads + hd, weight, tail)
            os_tx[s, qb] = jnp.transpose(tail)[0:8]
            for e in range(TB):
                bp = TB * qb + lax.rem(b + e, TB)
                if off == 0 and e == 0:
                    o_rx[s, b] = o_tx[s, pl.ds(pl.multiple_of(b * N, N), N), :]
                    os_rx[s, b] = os_tx[s, qb]
                    continue
                k, dev = off * TB + e, {"blk": bp}
                rdma(o_tx.at[s, pl.ds(bp * N, N), :], o_rx.at[s, b], o_send.at[s, k], o_recv.at[s, b], dev)
                rdma(os_tx.at[s, qb], os_rx.at[s, b], os_send.at[s, k], os_recv.at[s, b], dev)
        yield

        if s == 0:
            for k in range(1, H):
                _, dev = y_peer(k)
                rdma(cv_tx, cv_rx.at[h], cv_send.at[k], cv_recv.at[h], dev)

        for k in range(1, B):
            bp = lax.rem(b + k, B)
            arrived(os_rx.at[s, bp], os_recv.at[s, bp])
        for hd in range(heads):
            tops = [os_rx[s, bp, hd:hd + 1, :] for bp in range(B)]
            top = functools.reduce(jnp.maximum, tops)
            shares = [jnp.exp((tops[bp] - top) * scale) for bp in range(B)]
            den = shares[0] * os_rx[s, 0, heads + hd:heads + hd + 1, :]
            for bp in range(1, B):
                den = den + shares[bp] * os_rx[s, bp, heads + hd:heads + hd + 1, :]
            for bp in range(B):
                cf[hd * B + bp:hd * B + bp + 1, :] = shares[bp] / den
        cf_t[...] = jnp.transpose(cf[...])
        coef = cf_t[pl.ds(pl.multiple_of(lax.rem(b, TB) * N, N), N), :]
        for k in range(1, B):
            bp = lax.rem(b + k, B)
            arrived(o_rx.at[s, bp], o_recv.at[s, bp])
        pieces = []
        for hd in range(heads):
            cut = slice(128 * hd, 128 * (hd + 1))
            num = coef[:, hd * B:hd * B + 1] * o_rx[s, 0, :, cut].astype(F32)
            for bp in range(1, B):
                num = num + coef[:, hd * B + bp:hd * B + bp + 1] * o_rx[s, bp, :, cut].astype(F32)
            pieces.append(num)

        def ctx_rows(hp, lo, n):
            return ctx_rx.at[s, pl.ds(hp * N + lo, n), :]

        ctx_rx[s, pl.ds(pl.multiple_of(h * N, N), N), :] = jnp.concatenate(pieces, axis=1).astype(BF16)
        gather_start(ctx_rows, N, sems(cx_send, s), sems(cx_recv, s))
        yield
        gather_relay(ctx_rows, N, sems(cx_send, s), sems(cx_recv, s))
        yield
        if s == 0:
            local[3].wait()
            arrived(wo.at[1 - c], w_recv.at[1])
        gather_end(ctx_rows, N, sems(cx_recv, s))

        for cc in range(C):
            at_tx[s, cc] = jnp.dot(ctx_rx[s], wo[cc], preferred_element_type=F32).astype(BF16)
            to_owners(s, at_tx, at_rx, at_send, at_recv, cc)
        yield
        attended = from_owners(s, at_rx, at_recv)
        if s == 0:
            local[1].wait()
        mine = slice(s * N, (s + 1) * N)
        mix[mine, :] = tok_own[mine, :].astype(F32) + modv[2:3, own_cols] * attended
        mixed = mix[mine, :]

        mean_l = jnp.sum(mixed, -1, keepdims=True) * (1.0 / W)
        diff = mixed - mean_l
        n2_tx[s] = (diff * (1.0 + modv[4:5, own_cols])).astype(BF16)
        for up_ in range(U):
            rdma_or_local(
                jnp.logical_and(u == up_, c == uc),
                n2_tx.at[s], n2_rx.at[s, c, pl.ds(ui * N, N), :], n2_send.at[s, up_], n2_recv.at[s, c, ui],
                {"ulysses": up_, "tensor": h * C + uc},
            )
        m2_l = jnp.sum(diff * diff, -1, keepdims=True)
        lane_r = lax.broadcasted_iota(jnp.int32, (N, 128), 1)
        st2 = jnp.where(lane_r == 0, mean_l, jnp.where(lane_r == 1, m2_l, 0.0))
        st2_t = jnp.transpose(jnp.concatenate([st2, jnp.zeros((128 - N, 128), F32)], axis=0))[0:8]
        s2_tx[s] = st2_t
        s2_rx[s, t] = st2_t
        for k in range(1, T):
            rdma(s2_tx.at[s], s2_rx.at[s, t], s2_send.at[s, k], s2_recv.at[s, t], {"tensor": lax.rem(t + k, T)})
        yield
        for cc in range(C):
            for i in range(H):
                arrived(n2_rx.at[s, cc, pl.ds(i * N, N), :], n2_recv.at[s, cc, i])

        def act_rows(j):
            return lambda hp, lo, n: act_rx.at[s, j, pl.ds(hp * N + lo, n), :]

        for j in range(J):
            cut = slice(FW * j, FW * (j + 1))
            part = jnp.dot(n2_rx[s, 0], wu[0, :, cut], preferred_element_type=F32)
            part = part + jnp.dot(n2_rx[s, 1], wu[1, :, cut], preferred_element_type=F32)
            up_tx[s, j] = part.astype(BF16)
            scatter_start(up_tx.at[s, j], up_rb.at[s, j], N, sems(up_send, s, j), sems(up_recv, s, j))
        yield
        for k in range(1, T):
            tp = lax.rem(t + k, T)
            arrived(s2_rx.at[s, tp], s2_recv.at[s, tp])
        total = s2_rx[s, 0]
        for tp in range(1, T):
            total = total + s2_rx[s, tp]
        mean2 = total[0:1] * (1.0 / T)
        m2 = total[1:2]
        for tp in range(T):
            dev2 = s2_rx[s, tp, 0:1, :] - mean2
            m2 = m2 + W * dev2 * dev2
            fx_tx[s, tp:tp + 1, :] = dev2
        fx_tx[s, T:T + 1, :] = lax.rsqrt(m2 * (1.0 / features) + 1e-06)
        fx_tx[s, T + 1:16, :] = jnp.zeros((16 - T - 1, 128), F32)
        sends = u == c * H + h

        @pl.when(sends)
        def _():
            fx_rx[s] = fx_tx[s]
            for copy in fix_copies(s):
                copy.start()

        yield
        for j in range(J):
            scatter_relay(
                up_tx.at[s, j], up_rb.at[s, j], up_rx.at[s, j], N, sems(up_send, s, j), sems(up_recv, s, j)
            )
            yield
        for j in range(J):
            hidden = scatter_end(up_tx.at[s, j], up_rx.at[s, j], N, sems(up_recv, s, j))
            if j == 0:

                @pl.when(u != c * H + h)
                def _():
                    arrived(fx_rx.at[s], fx_recv.at[s])

                if s == 0:
                    for k in range(1, H):
                        hp, _ = y_peer(k)
                        arrived(cv_rx.at[hp], cv_recv.at[hp])
                fix = jnp.transpose(jnp.concatenate([fx_rx[s], jnp.zeros((112, 128), F32)], axis=0))[0:N]
            cut = slice(FW * j, FW * (j + 1))
            shifted = cv_rx[0, 2:3, cut]
            for hp in range(1, H):
                shifted = shifted + cv_rx[hp, 2:3, cut]
            for tp in range(T):
                hidden = hidden + fix[:, tp:tp + 1] * cv_rx[tp // C, tp % C:tp % C + 1, cut]
            hidden = fix[:, T:T + 1] * hidden + shifted
            act_rx[s, j, pl.ds(pl.multiple_of(h * N, N), N), :] = jax.nn.gelu(hidden, approximate=True).astype(BF16)
            gather_start(act_rows(j), N, sems(ac_send, s, j), sems(ac_recv, s, j))
            yield
        for j in range(J):
            gather_relay(act_rows(j), N, sems(ac_send, s, j), sems(ac_recv, s, j))
            yield
        if s == 0:
            local[5].wait()
            arrived(wd.at[1 - c], w_recv.at[3])
        accs = [None] * C
        for j in range(J):
            gather_end(act_rows(j), N, sems(ac_recv, s, j))
            for cc in range(C):
                part = jnp.dot(act_rx[s, j], wd[cc, FW * j:FW * (j + 1), :], preferred_element_type=F32)
                accs[cc] = part if j == 0 else accs[cc] + part
                if j == J - 1:
                    ff_tx[s, cc] = accs[cc].astype(BF16)
                    to_owners(s, ff_tx, ff_rx, ff_send, ff_recv, cc)
            yield
        feed = from_owners(s, ff_rx, ff_recv)
        out[mine, :] = mix[mine, :] + modv[5:6, own_cols] * feed

    steps = [part_steps(s) for s in range(S)]
    for s in ORDER:
        next(steps[s], None)

    for s in range(S):

        @pl.when(u == c * H + h)
        def _():
            for copy in fix_copies(s):
                copy.wait_send()

    for own, copy in pending:
        if own is None:
            copy.wait_send()
        else:
            pl.when(jnp.logical_not(own))(copy.wait_send)


def on_device(
    tokens, cond, mod_weight, qkv_weight, q_gain, k_gain, out_weight, up_weight, down_weight
):
    U = lax.axis_size("ulysses")
    B = lax.axis_size("blk")
    T = lax.axis_size("tensor")
    H = T // 2
    R, W = tokens.shape
    G = H * R
    FFL = up_weight.shape[1]
    J = 2
    S = 2
    N = R // S
    dma = pltpu.SemaphoreType.DMA
    vmem = pltpu.VMEM
    any_spec = pl.BlockSpec(memory_space=pltpu.HBM)
    vm_spec = pl.BlockSpec(memory_space=pltpu.VMEM)
    return pl.pallas_call(
        functools.partial(block_kernel, U, B, T),
        out_shape=jax.ShapeDtypeStruct((R, W), F32),
        in_specs=[any_spec] * 9,
        out_specs=vm_spec,
        scratch_shapes=[
            vmem((R, W), BF16),
            vmem((mod_weight.shape[0] // 128, 128), BF16),
            vmem((1, 128), F32),
            vmem((1, 128), F32),
            vmem((2, G, W), BF16),
            vmem((mod_weight.shape[1], mod_weight.shape[0]), BF16),
            vmem((3, 2, W, W), BF16),
            vmem((2, W, W), BF16),
            vmem((2, W, FFL), BF16),
            vmem((2, FFL, W), BF16),
            vmem((8, 128), F32),
            vmem((B, 8, 128), F32),
            vmem((24, 128), F32),
            vmem((T, 24, 128), F32),
            vmem((24, 128), F32),
            vmem((U, 24, 128), F32),
            vmem((8, 2 * W), F32),
            vmem((8, G), F32),
            vmem((H, 8, G), F32),
            vmem((3, G, W), BF16),
            vmem((3, 2, R // 2, W), BF16),
            vmem((3, 2, R, W), BF16),
            vmem((S, B * N, W), BF16),
            vmem((2, T * R, W), BF16),
            vmem((S, B * N, W), BF16),
            vmem((S, B, N, W), BF16),
            vmem((S, B * N // 128, 8, 128), F32),
            vmem((S, B, 8, 128), F32),
            vmem((128, 128), F32),
            vmem((128, 128), F32),
            vmem((S, H * N, W), BF16),
            vmem((S, 2, H * N, W), BF16),
            vmem((S, U, N, W), BF16),
            vmem((R, W), F32),
            vmem((S, 8, 128), F32),
            vmem((S, T, 8, 128), F32),
            vmem((S, 16, 128), F32),
            vmem((S, 16, 128), F32),
            vmem((8, FFL), F32),
            vmem((H, 8, FFL), F32),
            vmem((S, N, W), BF16),
            vmem((S, 2, H * N, W), BF16),
            vmem((S, J, H * N, FFL // J), BF16),
            vmem((S, J, 2, N // 2, FFL // J), BF16),
            vmem((S, J, 2, N, FFL // J), BF16),
            vmem((S, J, H * N, FFL // J), BF16),
            vmem((S, 2, H * N, W), BF16),
            vmem((S, U, N, W), BF16),
            dma((9,)), dma((4,)), dma((4,)),
            dma((U,)), dma((2, H)), dma((B,)), dma((B,)), dma((T,)), dma((T,)), dma((U,)), dma((U,)),
            dma((H,)), dma((H,)), dma((3, H)), dma((3, H)), dma((S, B)), dma((S, B)),
            dma((2, H)), dma((2, H)), dma((2, H)), dma((2, H)), dma((S, B)), dma((S, B)), dma((S, B)), dma((S, B)),
            dma((S, H)), dma((S, H)), dma((S, 2, H)), dma((S, U)), dma((S, T)), dma((S, T)), dma((S, U)), dma((S,)), dma((H,)), dma((H,)), dma((S, U)), dma((S, 2, H)),
            dma((S, J, H)), dma((S, J, H)), dma((S, J, H)), dma((S, J, H)), dma((S, 2, H)), dma((S, U)),
        ],
        compiler_params=pltpu.CompilerParams(
            collective_id=0, has_side_effects=True, vmem_limit_bytes=67043328
        ),
        name="block_kernel",
    )(
        tokens,
        cond.reshape(-1, 128),
        mod_weight.T,
        qkv_weight.transpose(1, 0, 2),
        q_gain.reshape(1, -1),
        k_gain.reshape(1, -1),
        out_weight,
        up_weight,
        down_weight,
    )


def solution(mesh):
    return jax.shard_map(
        on_device,
        mesh=mesh,
        in_specs=(
            P(("ulysses", "blk"), "tensor"),
            P(),
            P(None, ("ulysses", "blk", "tensor")),
            P("tensor", None, "ulysses"),
            P(),
            P(),
            P("ulysses", "tensor"),
            P("tensor", "ulysses"),
            P("ulysses", "tensor"),
        ),
        out_specs=P(("ulysses", "blk"), "tensor"),
        check_vma=False,
    )
```

```python
import functools
import math

import jax
import jax.numpy as jnp
from jax import lax
from jax.experimental import pallas as pl
from jax.experimental.pallas import tpu as pltpu
from jax.sharding import PartitionSpec as P

ORDER = [int(s) for s in "01001010101001010011010101011101"]
MESH = pl.DeviceIdType.MESH
F32 = jnp.float32
BF16 = jnp.bfloat16


def block_kernel(
    U, B, T,
    tokens, cond, mod_w, qkv_w, q_gain, k_gain, out_w, up_w, down_w,
    out,
    tok_own, cond_v, qg_v, kg_v, tok_rx, mw, wq, wo, wu, wd,
    m_tx, m_a, m_d, m_b, m_u, m_c, modv,
    st_tx, st_rx, rs_tx, rs_rb, rs_rx, q_rx, kv_rx, o_tx, o_rx, os_tx, os_rx, cf, cf_t, ctx_rx,
    at_tx, at_rx, mix, s2_tx, s2_rx, fx_tx, fx_rx, cv_tx, cv_rx, n2_tx, n2_rx, up_tx, up_rb, up_rx, act_rx, ff_tx, ff_rx,
    loc_sem, w_send, w_recv,
    tok_send, tok_recv, ma_send, ma_recv, mb_send, mb_recv, mc_send, mc_recv,
    st_send, st_recv, rs_send, rs_recv, q_send, q_recv, kv_send, kv_recv, km_send, km_recv, o_send, o_recv, os_send, os_recv,
    cx_send, cx_recv, at_send, at_recv, s2_send, s2_recv, fx_send, fx_recv, cv_send, cv_recv, n2_send, n2_recv,
    up_send, up_recv, ac_send, ac_recv, ff_send, ff_recv,
):
    C = 2
    H = T // C
    R, W = tokens.shape
    G = H * R
    S = 2
    N = R // S
    GN = H * N
    features = W * T
    u = lax.axis_index("ulysses")
    b = lax.axis_index("blk")
    t = lax.axis_index("tensor")
    h = t // C
    c = lax.rem(t, C)
    mate = {"tensor": h * C + (1 - c)}
    uc = u // H
    ui = lax.rem(u, H)
    pending = []

    def rdma(src, dst, send, recv, dev):
        copy = pltpu.make_async_remote_copy(
            src_ref=src, dst_ref=dst, send_sem=send, recv_sem=recv,
            device_id=dev, device_id_type=MESH,
        )
        copy.start()
        pending.append((None, copy))

    def rdma_or_local(own, src, dst, send, recv, dev):
        copy = pltpu.make_async_remote_copy(
            src_ref=src, dst_ref=dst, send_sem=send, recv_sem=recv,
            device_id=dev, device_id_type=MESH,
        )

        @pl.when(own)
        def _():
            pltpu.make_async_copy(src, dst, recv).start()

        @pl.when(jnp.logical_not(own))
        def _():
            copy.start()

        pending.append((own, copy))

    def arrived(dst, recv):
        pltpu.make_async_copy(dst, dst, recv).wait()

    def y_peer(k):
        hp = lax.rem(h + k, H)
        return hp, {"tensor": hp * C + c}

    hr, right = y_peer(1)
    ho, _ = y_peer(2)
    hl, left = y_peer(3)

    def gather_start(rows, n, send, recv):
        mine = rows(h, 0, n)
        rdma(mine, mine, send(0), recv(0), right)
        rdma(mine, mine, send(1), recv(1), left)

    def gather_relay(rows, n, send, recv):
        half = n // 2
        arrived(rows(hl, 0, n), recv(0))
        part = rows(hl, 0, half)
        rdma(part, part, send(2), recv(2), right)
        arrived(rows(hr, 0, n), recv(1))
        part = rows(hr, half, half)
        rdma(part, part, send(3), recv(3), left)

    def gather_end(rows, n, recv):
        half = n // 2
        arrived(rows(ho, 0, half), recv(2))
        arrived(rows(ho, half, half), recv(3))

    def scatter_start(tx, rb, rx, n, send, recv):
        half = n // 2
        rdma(tx.at[pl.ds(ho * n, half), :], rb.at[0], send(0), recv(0), right)
        rdma(tx.at[pl.ds(ho * n + half, half), :], rb.at[1], send(1), recv(1), left)
        for side, (to, dev) in enumerate(((hr, right), (hl, left))):
            lo = (1 - side) * half
            rdma(
                tx.at[pl.ds(to * n + lo, half), :], rx.at[side, pl.ds(lo, half), :],
                send(4 + side), recv(4 + side), dev,
            )

    def scatter_relay(tx, rb, rx, n, send, recv):
        half = n // 2
        for side, (to, dev) in enumerate(((hr, right), (hl, left))):
            arrived(rb.at[side], recv(side))
            at = pl.ds(pl.multiple_of(to * n + side * half, half), half)
            tx[at, :] = (tx[at, :].astype(F32) + rb[side].astype(F32)).astype(BF16)
            rdma(
                tx.at[pl.ds(to * n + side * half, half), :], rx.at[side, pl.ds(side * half, half), :],
                send(2 + side), recv(2 + side), dev,
            )

    def scatter_end(tx, rx, n, recv):
        half = n // 2
        for side in range(2):
            arrived(rx.at[side, pl.ds((1 - side) * half, half), :], recv(4 + side))
            arrived(rx.at[side, pl.ds(side * half, half), :], recv(2 + side))
        own = tx[pl.ds(pl.multiple_of(h * n, n), n), :].astype(F32)
        return own + rx[0].astype(F32) + rx[1].astype(F32)

    barrier = pltpu.get_barrier_semaphore()
    count = 0
    for k in range(1, B):
        pl.semaphore_signal(barrier, inc=1, device_id={"blk": lax.rem(b + k, B)}, device_id_type=MESH)
        count += 1
    for k in range(1, T):
        pl.semaphore_signal(barrier, inc=1, device_id={"tensor": lax.rem(t + k, T)}, device_id_type=MESH)
        count += 1
    for k in range(1, U):
        for cc in range(C):
            pl.semaphore_signal(
                barrier, inc=1,
                device_id={"ulysses": lax.rem(u + k, U), "tensor": h * C + cc},
                device_id_type=MESH,
            )
            count += 1

    local = [
        pltpu.make_async_copy(mod_w, mw, loc_sem.at[0]),
        pltpu.make_async_copy(tokens, tok_own, loc_sem.at[1]),
        pltpu.make_async_copy(qkv_w, wq.at[:, c], loc_sem.at[2]),
        pltpu.make_async_copy(out_w, wo.at[c], loc_sem.at[3]),
        pltpu.make_async_copy(up_w, wu.at[c], loc_sem.at[4]),
        pltpu.make_async_copy(down_w, wd.at[c], loc_sem.at[5]),
        pltpu.make_async_copy(cond, cond_v, loc_sem.at[6]),
        pltpu.make_async_copy(q_gain, qg_v, loc_sem.at[7]),
        pltpu.make_async_copy(k_gain, kg_v, loc_sem.at[8]),
    ]
    for copy in local:
        copy.start()

    cf[...] = jnp.zeros_like(cf)
    local[6].wait()
    condf = cond_v[...].astype(F32)
    active = condf * jax.nn.sigmoid(condf)
    active = jnp.concatenate([active[i:i + 1] for i in range(features // 128)], axis=1).astype(BF16)
    local[0].wait()
    share = lax.dot_general(
        jnp.broadcast_to(active, (16, features)), mw[...],
        (((1,), (1,)), ((), ())), preferred_element_type=F32,
    )
    n_share = mod_w.shape[0]
    start = n_share * (b * T + t)
    lanes2 = lax.broadcasted_iota(jnp.int32, (n_share, 256), 1)
    rows2 = lax.broadcasted_iota(jnp.int32, (n_share, 256), 0)
    place = (lanes2 == rows2 + lax.rem(start, 128)).astype(F32)
    placed = jnp.dot(share[0:8], place, preferred_element_type=F32, precision=lax.Precision.HIGHEST)
    sub8 = lax.broadcasted_iota(jnp.int32, (8, 128), 0)
    tile = jnp.where(sub8 == 0, placed[:, 0:128], jnp.where(sub8 == 1, placed[:, 128:256], 0.0))
    m_tx[...] = tile
    m_a[b] = tile

    pl.semaphore_wait(barrier, count)

    for k in range(1, B):
        rdma(m_tx, m_a.at[b], ma_send.at[k], ma_recv.at[b], {"blk": lax.rem(b + k, B)})
    for up_ in range(U):
        rdma_or_local(
            jnp.logical_and(u == up_, c == uc),
            tokens, tok_rx.at[c, pl.ds(ui * R, R), :], tok_send.at[up_], tok_recv.at[c, ui],
            {"ulysses": up_, "tensor": h * C + uc},
        )
    rdma(qkv_w, wq.at[:, c], w_send.at[0], w_recv.at[0], mate)
    rdma(out_w, wo.at[c], w_send.at[1], w_recv.at[1], mate)
    rdma(up_w, wu.at[c], w_send.at[2], w_recv.at[2], mate)
    rdma(down_w, wd.at[c], w_send.at[3], w_recv.at[3], mate)

    per_u = n_share * B * T // 128
    m_d[...] = jnp.zeros_like(m_d)
    for k in range(B):
        if k:
            bp = lax.rem(b + k, B)
            arrived(m_a.at[bp], ma_recv.at[bp])
    for bp in range(B):
        row = (n_share * (bp * T + t)) // 128
        m_d[pl.ds(row, 1), :] += m_a[bp, 0:1, :]
        m_d[pl.ds(row + 1, 1), :] += m_a[bp, 1:2, :]
    m_b[t] = m_d[...]
    for k in range(1, T):
        rdma(m_d, m_b.at[t], mb_send.at[k], mb_recv.at[t], {"tensor": lax.rem(t + k, T)})

    for cc in range(C):
        for i in range(H):
            arrived(tok_rx.at[cc, pl.ds(i * R, R), :], tok_recv.at[cc, i])
    x0 = tok_rx[0].astype(F32)
    x1 = tok_rx[1].astype(F32)
    local_mean = (jnp.sum(x0, -1, keepdims=True) + jnp.sum(x1, -1, keepdims=True)) * (1.0 / (C * W))
    d0 = x0 - local_mean
    d1 = x1 - local_mean
    local_m2 = jnp.sum(d0 * d0, -1, keepdims=True) + jnp.sum(d1 * d1, -1, keepdims=True)
    lane = lax.broadcasted_iota(jnp.int32, (G, 128), 1)
    stats = jnp.where(lane == 0, local_mean, jnp.where(lane == 1, local_m2, 0.0))
    stats_t = jnp.transpose(stats)[0:8]
    st_tx[...] = stats_t
    st_rx[h] = stats_t
    for k in range(1, H):
        hp, dev = y_peer(k)
        rdma(st_tx, st_rx.at[h], st_send.at[k], st_recv.at[h], dev)

    for k in range(1, T):
        tp = lax.rem(t + k, T)
        arrived(m_b.at[tp], mb_recv.at[tp])
    dense = m_b[0]
    for tp in range(1, T):
        dense = dense + m_b[tp]
    m_u[...] = dense
    m_c[u] = dense
    for k in range(1, U):
        rdma(m_u, m_c.at[u], mc_send.at[k], mc_recv.at[u], {"ulysses": lax.rem(u + k, U)})

    for k in range(1, H):
        hp, _ = y_peer(k)
        arrived(st_rx.at[hp], st_recv.at[hp])
    mean = st_rx[0, 0:1, :]
    for hp in range(1, H):
        mean = mean + st_rx[hp, 0:1, :]
    mean = mean * (1.0 / H)
    m2 = jnp.zeros_like(mean)
    for hp in range(H):
        diff = st_rx[hp, 0:1, :] - mean
        m2 = m2 + st_rx[hp, 1:2, :] + (C * W) * diff * diff
    rstd = lax.rsqrt(m2 * (1.0 / features) + 1e-06)
    subg = lax.broadcasted_iota(jnp.int32, (128, G), 0)
    cols = jnp.transpose(jnp.where(subg == 0, mean, jnp.where(subg == 1, rstd, 0.0)))
    mean_c, rstd_c = cols[:, 0:1], cols[:, 1:2]

    for k in range(1, U):
        upk = lax.rem(u + k, U)
        arrived(m_c.at[upk], mc_recv.at[upk])
    for v in range(6):
        for k in range(C * W // 128):
            row = v * (features // 128) + h * (C * W // 128) + k
            modv[v:v + 1, 128 * k:128 * (k + 1)] = m_c[row // per_u, pl.ds(lax.rem(row, per_u), 1), :]

    n0 = ((x0 - mean_c) * rstd_c * (1.0 + modv[1:2, 0:W]) + modv[0:1, 0:W]).astype(BF16)
    n1 = ((x1 - mean_c) * rstd_c * (1.0 + modv[1:2, W:2 * W]) + modv[0:1, W:2 * W]).astype(BF16)

    local[2].wait()
    arrived(wq.at[:, 1 - c], w_recv.at[0])
    def rs_sems(sems, g):
        return lambda k: sems.at[g, k]

    for g in range(3):
        part = jnp.dot(n0, wq[g, 0], preferred_element_type=F32)
        part = part + jnp.dot(n1, wq[g, 1], preferred_element_type=F32)
        rs_tx[g] = part.astype(BF16)
        scatter_start(rs_tx.at[g], rs_rb.at[g], rs_rx.at[g], R, rs_sems(rs_send, g), rs_sems(rs_recv, g))

    heads = W // 128

    def proj_relay(g):
        scatter_relay(rs_tx.at[g], rs_rb.at[g], rs_rx.at[g], R, rs_sems(rs_send, g), rs_sems(rs_recv, g))

    def kv_rows(g):
        return lambda hp, lo, n: kv_rx.at[g, pl.ds((c * H + hp) * R + lo, n), :]

    def to_mate(g, hp, i):
        rows = kv_rows(g)(hp, 0, R)
        rdma(rows, rows, km_send.at[g, i], km_recv.at[g, hp], mate)

    def proj_end(g):
        total = scatter_end(rs_tx.at[g], rs_rx.at[g], R, rs_sems(rs_recv, g))
        if g < 2:
            local[7 + g].wait()
            gain = (qg_v if g == 0 else kg_v)[...]
            pieces = []
            for hd in range(heads):
                piece = total[:, 128 * hd:128 * (hd + 1)]
                ms = jnp.mean(piece * piece, axis=-1, keepdims=True)
                pieces.append(piece * lax.rsqrt(ms + 1e-06) * gain)
            total = jnp.concatenate(pieces, axis=1)
        if g == 0:
            for s in range(S):
                q_rx[s, pl.ds(pl.multiple_of(b * N, N), N), :] = total[s * N:(s + 1) * N].astype(BF16)
                rows = q_rx.at[s, pl.ds(b * N, N), :]
                for k in sorted(range(1, B), key=lambda k: -min(k, B - k)):
                    rdma(rows, rows, q_send.at[s, k], q_recv.at[s, b], {"blk": lax.rem(b + k, B)})
        else:
            kv_rx[g - 1, pl.ds(pl.multiple_of((c * H + h) * R, R), R), :] = total.astype(BF16)
            gather_start(kv_rows(g - 1), R, rs_sems(kv_send, g - 1), rs_sems(kv_recv, g - 1))
            to_mate(g - 1, h, 0)

    local[4].wait()
    arrived(wu.at[1 - c], w_recv.at[2])
    for cc in range(C):
        cut = slice(cc * W, (cc + 1) * W)
        vecs = []
        for vec in (1.0 + modv[4:5, cut], modv[3:4, cut]):
            high = vec.astype(BF16).astype(F32)
            vecs += [high, vec - high]
        sub16 = lax.broadcasted_iota(jnp.int32, (16, W), 0)
        left_side = jnp.zeros((16, W), F32)
        for i, vec in enumerate(vecs):
            left_side = jnp.where(sub16 == i, vec, left_side)
        cols16 = jnp.dot(left_side.astype(BF16), wu[cc], preferred_element_type=F32)
        cv_tx[cc:cc + 1, :] = cols16[0:1] + cols16[1:2]
        shifted = cols16[2:3] + cols16[3:4]
        cv_tx[2:3, :] = shifted if cc == 0 else cv_tx[2:3, :] + shifted
    cv_tx[3:8, :] = jnp.zeros((5, wu.shape[2]), F32)
    cv_rx[h] = cv_tx[...]

    proj_relay(0)
    proj_relay(1)
    proj_end(0)
    proj_relay(2)
    proj_end(1)
    proj_end(2)
    for g in range(2):
        gather_relay(kv_rows(g), R, rs_sems(kv_send, g), rs_sems(kv_recv, g))
        to_mate(g, hl, 1)
        to_mate(g, hr, 2)
    for g in range(2):
        gather_end(kv_rows(g), R, rs_sems(kv_recv, g))
        to_mate(g, ho, 3)
    for k in range(1, B):
        bp = lax.rem(b + k, B)
        for s in range(S):
            arrived(q_rx.at[s, pl.ds(bp * N, N), :], q_recv.at[s, bp])
    for g in range(2):
        for hp in range(H):
            arrived(kv_rx.at[g, pl.ds(((1 - c) * H + hp) * R, R), :], km_recv.at[g, hp])

    scale = 1.0 / math.sqrt(128)
    TB = 128 // N
    nq = B // TB
    own_cols = pl.ds(pl.multiple_of(c * W, 128), W)
    J, FW = up_tx.shape[1], up_tx.shape[3]

    def sems(ref, *index):
        return lambda k: ref.at[(*index, k)]

    def to_owners(s, tx, rx, send, recv, cc):
        for hp in range(H):
            up_ = c * H + hp
            rdma_or_local(
                jnp.logical_and(up_ == u, c == cc),
                tx.at[s, cc, pl.ds(hp * N, N), :], rx.at[s, u], send.at[s, cc, hp], recv.at[s, u],
                {"ulysses": up_, "tensor": h * C + cc},
            )

    def from_owners(s, rx, recv):
        for up_ in range(U):
            arrived(rx.at[s, up_], recv.at[s, up_])
        total = rx[s, 0].astype(F32)
        for up_ in range(1, U):
            total = total + rx[s, up_].astype(F32)
        return total

    def fix_copies(s):
        return [
            pltpu.make_async_remote_copy(
                src_ref=fx_tx.at[s], dst_ref=fx_rx.at[s], send_sem=fx_send.at[s, k], recv_sem=fx_recv.at[s],
                device_id={"ulysses": lax.rem(u + k, U)}, device_id_type=MESH,
            )
            for k in range(1, U)
        ]

    def part_steps(s):
        for off in range(nq - 1, -1, -1):
            qb = lax.rem(b // TB + off, nq)
            at = pl.multiple_of(qb * 128, 128)
            lane_q = lax.broadcasted_iota(jnp.int32, (128, 128), 1)
            tail = jnp.zeros((128, 128), F32)
            for hd in range(heads):
                cut = slice(128 * hd, 128 * (hd + 1))
                score = lax.dot_general(
                    q_rx[s, pl.ds(at, 128), cut], kv_rx[0, :, cut],
                    (((1,), (1,)), ((), ())), preferred_element_type=F32,
                )
                top = jnp.max(score, axis=-1, keepdims=True)
                p = jnp.exp((score - top) * scale)
                weight = jnp.sum(p, axis=-1, keepdims=True)
                o = jnp.dot(p.astype(BF16), kv_rx[1, :, cut], preferred_element_type=F32)
                o_tx[s, pl.ds(at, 128), cut] = o.astype(BF16)
                tail = jnp.where(lane_q == hd, top, tail)
                tail = jnp.where(lane_q == heads + hd, weight, tail)
            os_tx[s, qb] = jnp.transpose(tail)[0:8]
            for e in range(TB):
                bp = TB * qb + lax.rem(b + e, TB)
                if off == 0 and e == 0:
                    o_rx[s, b] = o_tx[s, pl.ds(pl.multiple_of(b * N, N), N), :]
                    os_rx[s, b] = os_tx[s, qb]
                    continue
                k, dev = off * TB + e, {"blk": bp}
                rdma(o_tx.at[s, pl.ds(bp * N, N), :], o_rx.at[s, b], o_send.at[s, k], o_recv.at[s, b], dev)
                rdma(os_tx.at[s, qb], os_rx.at[s, b], os_send.at[s, k], os_recv.at[s, b], dev)
        yield

        if s == 0:
            for k in range(1, H):
                _, dev = y_peer(k)
                rdma(cv_tx, cv_rx.at[h], cv_send.at[k], cv_recv.at[h], dev)

        for k in range(1, B):
            bp = lax.rem(b + k, B)
            arrived(os_rx.at[s, bp], os_recv.at[s, bp])
        for hd in range(heads):
            tops = [os_rx[s, bp, hd:hd + 1, :] for bp in range(B)]
            top = functools.reduce(jnp.maximum, tops)
            shares = [jnp.exp((tops[bp] - top) * scale) for bp in range(B)]
            den = shares[0] * os_rx[s, 0, heads + hd:heads + hd + 1, :]
            for bp in range(1, B):
                den = den + shares[bp] * os_rx[s, bp, heads + hd:heads + hd + 1, :]
            for bp in range(B):
                cf[hd * B + bp:hd * B + bp + 1, :] = shares[bp] / den
        cf_t[...] = jnp.transpose(cf[...])
        coef = cf_t[pl.ds(pl.multiple_of(lax.rem(b, TB) * N, N), N), :]
        for k in range(1, B):
            bp = lax.rem(b + k, B)
            arrived(o_rx.at[s, bp], o_recv.at[s, bp])
        pieces = []
        for hd in range(heads):
            cut = slice(128 * hd, 128 * (hd + 1))
            num = coef[:, hd * B:hd * B + 1] * o_rx[s, 0, :, cut].astype(F32)
            for bp in range(1, B):
                num = num + coef[:, hd * B + bp:hd * B + bp + 1] * o_rx[s, bp, :, cut].astype(F32)
            pieces.append(num)

        def ctx_rows(hp, lo, n):
            return ctx_rx.at[s, pl.ds(hp * N + lo, n), :]

        ctx_rx[s, pl.ds(pl.multiple_of(h * N, N), N), :] = jnp.concatenate(pieces, axis=1).astype(BF16)
        gather_start(ctx_rows, N, sems(cx_send, s), sems(cx_recv, s))
        yield
        gather_relay(ctx_rows, N, sems(cx_send, s), sems(cx_recv, s))
        yield
        if s == 0:
            local[3].wait()
            arrived(wo.at[1 - c], w_recv.at[1])
        gather_end(ctx_rows, N, sems(cx_recv, s))

        for cc in range(C):
            at_tx[s, cc] = jnp.dot(ctx_rx[s], wo[cc], preferred_element_type=F32).astype(BF16)
            to_owners(s, at_tx, at_rx, at_send, at_recv, cc)
        yield
        attended = from_owners(s, at_rx, at_recv)
        if s == 0:
            local[1].wait()
        mine = slice(s * N, (s + 1) * N)
        mix[mine, :] = tok_own[mine, :].astype(F32) + modv[2:3, own_cols] * attended
        mixed = mix[mine, :]

        mean_l = jnp.sum(mixed, -1, keepdims=True) * (1.0 / W)
        diff = mixed - mean_l
        n2_tx[s] = (diff * (1.0 + modv[4:5, own_cols])).astype(BF16)
        for up_ in range(U):
            rdma_or_local(
                jnp.logical_and(u == up_, c == uc),
                n2_tx.at[s], n2_rx.at[s, c, pl.ds(ui * N, N), :], n2_send.at[s, up_], n2_recv.at[s, c, ui],
                {"ulysses": up_, "tensor": h * C + uc},
            )
        m2_l = jnp.sum(diff * diff, -1, keepdims=True)
        lane_r = lax.broadcasted_iota(jnp.int32, (N, 128), 1)
        st2 = jnp.where(lane_r == 0, mean_l, jnp.where(lane_r == 1, m2_l, 0.0))
        st2_t = jnp.transpose(jnp.concatenate([st2, jnp.zeros((128 - N, 128), F32)], axis=0))[0:8]
        s2_tx[s] = st2_t
        s2_rx[s, t] = st2_t
        for k in range(1, T):
            rdma(s2_tx.at[s], s2_rx.at[s, t], s2_send.at[s, k], s2_recv.at[s, t], {"tensor": lax.rem(t + k, T)})
        yield
        for cc in range(C):
            for i in range(H):
                arrived(n2_rx.at[s, cc, pl.ds(i * N, N), :], n2_recv.at[s, cc, i])

        def act_rows(j):
            return lambda hp, lo, n: act_rx.at[s, j, pl.ds(hp * N + lo, n), :]

        for j in range(J):
            cut = slice(FW * j, FW * (j + 1))
            part = jnp.dot(n2_rx[s, 0], wu[0, :, cut], preferred_element_type=F32)
            part = part + jnp.dot(n2_rx[s, 1], wu[1, :, cut], preferred_element_type=F32)
            up_tx[s, j] = part.astype(BF16)
            scatter_start(up_tx.at[s, j], up_rb.at[s, j], up_rx.at[s, j], N, sems(up_send, s, j), sems(up_recv, s, j))
        yield
        for k in range(1, T):
            tp = lax.rem(t + k, T)
            arrived(s2_rx.at[s, tp], s2_recv.at[s, tp])
        total = s2_rx[s, 0]
        for tp in range(1, T):
            total = total + s2_rx[s, tp]
        mean2 = total[0:1] * (1.0 / T)
        m2 = total[1:2]
        for tp in range(T):
            dev2 = s2_rx[s, tp, 0:1, :] - mean2
            m2 = m2 + W * dev2 * dev2
            fx_tx[s, tp:tp + 1, :] = dev2
        fx_tx[s, T:T + 1, :] = lax.rsqrt(m2 * (1.0 / features) + 1e-06)
        fx_tx[s, T + 1:16, :] = jnp.zeros((16 - T - 1, 128), F32)
        sends = u == c * H + h

        @pl.when(sends)
        def _():
            fx_rx[s] = fx_tx[s]
            for copy in fix_copies(s):
                copy.start()

        yield
        for j in range(J):
            scatter_relay(
                up_tx.at[s, j], up_rb.at[s, j], up_rx.at[s, j], N, sems(up_send, s, j), sems(up_recv, s, j)
            )
            yield
        for j in range(J):
            hidden = scatter_end(up_tx.at[s, j], up_rx.at[s, j], N, sems(up_recv, s, j))
            if j == 0:

                @pl.when(u != c * H + h)
                def _():
                    arrived(fx_rx.at[s], fx_recv.at[s])

                if s == 0:
                    for k in range(1, H):
                        hp, _ = y_peer(k)
                        arrived(cv_rx.at[hp], cv_recv.at[hp])
                fix = jnp.transpose(jnp.concatenate([fx_rx[s], jnp.zeros((112, 128), F32)], axis=0))[0:N]
            cut = slice(FW * j, FW * (j + 1))
            shifted = cv_rx[0, 2:3, cut]
            for hp in range(1, H):
                shifted = shifted + cv_rx[hp, 2:3, cut]
            for tp in range(T):
                hidden = hidden + fix[:, tp:tp + 1] * cv_rx[tp // C, tp % C:tp % C + 1, cut]
            hidden = fix[:, T:T + 1] * hidden + shifted
            act_rx[s, j, pl.ds(pl.multiple_of(h * N, N), N), :] = jax.nn.gelu(hidden, approximate=True).astype(BF16)
            gather_start(act_rows(j), N, sems(ac_send, s, j), sems(ac_recv, s, j))
            yield
        for j in range(J):
            gather_relay(act_rows(j), N, sems(ac_send, s, j), sems(ac_recv, s, j))
            yield
        if s == 0:
            local[5].wait()
            arrived(wd.at[1 - c], w_recv.at[3])
        accs = [None] * C
        for j in range(J):
            gather_end(act_rows(j), N, sems(ac_recv, s, j))
            for cc in range(C):
                part = jnp.dot(act_rx[s, j], wd[cc, FW * j:FW * (j + 1), :], preferred_element_type=F32)
                accs[cc] = part if j == 0 else accs[cc] + part
                if j == J - 1:
                    ff_tx[s, cc] = accs[cc].astype(BF16)
                    to_owners(s, ff_tx, ff_rx, ff_send, ff_recv, cc)
            yield
        feed = from_owners(s, ff_rx, ff_recv)
        out[mine, :] = mix[mine, :] + modv[5:6, own_cols] * feed

    steps = [part_steps(s) for s in range(S)]
    for s in ORDER:
        next(steps[s], None)

    for s in range(S):

        @pl.when(u == c * H + h)
        def _():
            for copy in fix_copies(s):
                copy.wait_send()

    for own, copy in pending:
        if own is None:
            copy.wait_send()
        else:
            pl.when(jnp.logical_not(own))(copy.wait_send)


def on_device(
    tokens, cond, mod_weight, qkv_weight, q_gain, k_gain, out_weight, up_weight, down_weight
):
    U = lax.axis_size("ulysses")
    B = lax.axis_size("blk")
    T = lax.axis_size("tensor")
    H = T // 2
    R, W = tokens.shape
    G = H * R
    FFL = up_weight.shape[1]
    J = 2
    S = 2
    N = R // S
    dma = pltpu.SemaphoreType.DMA
    vmem = pltpu.VMEM
    any_spec = pl.BlockSpec(memory_space=pltpu.HBM)
    vm_spec = pl.BlockSpec(memory_space=pltpu.VMEM)
    return pl.pallas_call(
        functools.partial(block_kernel, U, B, T),
        out_shape=jax.ShapeDtypeStruct((R, W), F32),
        in_specs=[any_spec] * 9,
        out_specs=vm_spec,
        scratch_shapes=[
            vmem((R, W), BF16),
            vmem((mod_weight.shape[0] // 128, 128), BF16),
            vmem((1, 128), F32),
            vmem((1, 128), F32),
            vmem((2, G, W), BF16),
            vmem((mod_weight.shape[1], mod_weight.shape[0]), BF16),
            vmem((3, 2, W, W), BF16),
            vmem((2, W, W), BF16),
            vmem((2, W, FFL), BF16),
            vmem((2, FFL, W), BF16),
            vmem((8, 128), F32),
            vmem((B, 8, 128), F32),
            vmem((24, 128), F32),
            vmem((T, 24, 128), F32),
            vmem((24, 128), F32),
            vmem((U, 24, 128), F32),
            vmem((8, 2 * W), F32),
            vmem((8, G), F32),
            vmem((H, 8, G), F32),
            vmem((3, G, W), BF16),
            vmem((3, 2, R // 2, W), BF16),
            vmem((3, 2, R, W), BF16),
            vmem((S, B * N, W), BF16),
            vmem((2, T * R, W), BF16),
            vmem((S, B * N, W), BF16),
            vmem((S, B, N, W), BF16),
            vmem((S, B * N // 128, 8, 128), F32),
            vmem((S, B, 8, 128), F32),
            vmem((128, 128), F32),
            vmem((128, 128), F32),
            vmem((S, H * N, W), BF16),
            vmem((S, 2, H * N, W), BF16),
            vmem((S, U, N, W), BF16),
            vmem((R, W), F32),
            vmem((S, 8, 128), F32),
            vmem((S, T, 8, 128), F32),
            vmem((S, 16, 128), F32),
            vmem((S, 16, 128), F32),
            vmem((8, FFL), F32),
            vmem((H, 8, FFL), F32),
            vmem((S, N, W), BF16),
            vmem((S, 2, H * N, W), BF16),
            vmem((S, J, H * N, FFL // J), BF16),
            vmem((S, J, 2, N // 2, FFL // J), BF16),
            vmem((S, J, 2, N, FFL // J), BF16),
            vmem((S, J, H * N, FFL // J), BF16),
            vmem((S, 2, H * N, W), BF16),
            vmem((S, U, N, W), BF16),
            dma((9,)), dma((4,)), dma((4,)),
            dma((U,)), dma((2, H)), dma((B,)), dma((B,)), dma((T,)), dma((T,)), dma((U,)), dma((U,)),
            dma((H,)), dma((H,)), dma((3, 6)), dma((3, 6)), dma((S, B)), dma((S, B)),
            dma((2, H)), dma((2, H)), dma((2, H)), dma((2, H)), dma((S, B)), dma((S, B)), dma((S, B)), dma((S, B)),
            dma((S, H)), dma((S, H)), dma((S, 2, H)), dma((S, U)), dma((S, T)), dma((S, T)), dma((S, U)), dma((S,)), dma((H,)), dma((H,)), dma((S, U)), dma((S, 2, H)),
            dma((S, J, 6)), dma((S, J, 6)), dma((S, J, H)), dma((S, J, H)), dma((S, 2, H)), dma((S, U)),
        ],
        compiler_params=pltpu.CompilerParams(
            collective_id=0, has_side_effects=True, vmem_limit_bytes=67043328
        ),
        name="block_kernel",
    )(
        tokens,
        cond.reshape(-1, 128),
        mod_weight.T,
        qkv_weight.transpose(1, 0, 2),
        q_gain.reshape(1, -1),
        k_gain.reshape(1, -1),
        out_weight,
        up_weight,
        down_weight,
    )


def solution(mesh):
    return jax.shard_map(
        on_device,
        mesh=mesh,
        in_specs=(
            P(("ulysses", "blk"), "tensor"),
            P(),
            P(None, ("ulysses", "blk", "tensor")),
            P("tensor", None, "ulysses"),
            P(),
            P(),
            P("ulysses", "tensor"),
            P("tensor", "ulysses"),
            P("ulysses", "tensor"),
        ),
        out_specs=P(("ulysses", "blk"), "tensor"),
        check_vma=False,
    )
```

```python
import functools
import math

import jax
import jax.numpy as jnp
from jax import lax
from jax.experimental import pallas as pl
from jax.experimental.pallas import tpu as pltpu
from jax.sharding import PartitionSpec as P

ORDER = [int(s) for s in "01001011010010100101010101011101"]
MESH = pl.DeviceIdType.MESH
F32 = jnp.float32
BF16 = jnp.bfloat16


def block_kernel(
    U, B, T,
    tokens, cond, mod_w, qkv_w, q_gain, k_gain, out_w, up_w, down_w,
    out,
    tok_own, cond_v, qg_v, kg_v, tok_rx, mw, wq, wo, wu, wd,
    m_tx, m_a, m_d, m_b, m_u, m_c, modv,
    st_tx, st_rx, rs_tx, rs_rb, rs_rx, q_rx, kv_rx, o_tx, o_rx, os_tx, os_rx, cf, cf_t, ctx_rx,
    at_tx, at_rx, mix, s2_tx, s2_rx, fx_tx, fx_rx, cv_tx, cv_rx, n2_tx, n2_rx, up_tx, up_rb, up_rx, act_rx, ff_tx, ff_rx,
    loc_sem, w_send, w_recv,
    tok_send, tok_recv, ma_send, ma_recv, mb_send, mb_recv, mc_send, mc_recv,
    st_send, st_recv, rs_send, rs_recv, q_send, q_recv, kv_send, kv_recv, km_send, km_recv, o_send, o_recv, os_send, os_recv,
    cx_send, cx_recv, at_send, at_recv, s2_send, s2_recv, fx_send, fx_recv, cv_send, cv_recv, n2_send, n2_recv,
    up_send, up_recv, ac_send, ac_recv, ff_send, ff_recv,
):
    C = 2
    H = T // C
    R, W = tokens.shape
    G = H * R
    S = 2
    N = R // S
    GN = H * N
    features = W * T
    u = lax.axis_index("ulysses")
    b = lax.axis_index("blk")
    t = lax.axis_index("tensor")
    h = t // C
    c = lax.rem(t, C)
    mate = {"tensor": h * C + (1 - c)}
    uc = u // H
    ui = lax.rem(u, H)
    pending = []

    def rdma(src, dst, send, recv, dev):
        copy = pltpu.make_async_remote_copy(
            src_ref=src, dst_ref=dst, send_sem=send, recv_sem=recv,
            device_id=dev, device_id_type=MESH,
        )
        copy.start()
        pending.append((None, copy))

    def rdma_or_local(own, src, dst, send, recv, dev):
        copy = pltpu.make_async_remote_copy(
            src_ref=src, dst_ref=dst, send_sem=send, recv_sem=recv,
            device_id=dev, device_id_type=MESH,
        )

        @pl.when(own)
        def _():
            pltpu.make_async_copy(src, dst, recv).start()

        @pl.when(jnp.logical_not(own))
        def _():
            copy.start()

        pending.append((own, copy))

    def arrived(dst, recv):
        pltpu.make_async_copy(dst, dst, recv).wait()

    def y_peer(k):
        hp = lax.rem(h + k, H)
        return hp, {"tensor": hp * C + c}

    hr, right = y_peer(1)
    ho, _ = y_peer(2)
    hl, left = y_peer(3)

    def gather_start(rows, n, send, recv):
        mine = rows(h, 0, n)
        rdma(mine, mine, send(0), recv(0), right)
        rdma(mine, mine, send(1), recv(1), left)

    def gather_relay(rows, n, send, recv):
        half = n // 2
        arrived(rows(hl, 0, n), recv(0))
        part = rows(hl, 0, half)
        rdma(part, part, send(2), recv(2), right)
        arrived(rows(hr, 0, n), recv(1))
        part = rows(hr, half, half)
        rdma(part, part, send(3), recv(3), left)

    def gather_end(rows, n, recv):
        half = n // 2
        arrived(rows(ho, 0, half), recv(2))
        arrived(rows(ho, half, half), recv(3))

    def scatter_start(tx, rb, n, send, recv):
        half = n // 2
        rdma(tx.at[pl.ds(ho * n, half), :], rb.at[0], send(0), recv(0), right)
        rdma(tx.at[pl.ds(ho * n + half, half), :], rb.at[1], send(1), recv(1), left)

    def scatter_relay(tx, rb, rx, n, send, recv):
        half = n // 2
        for side, (to, dev) in enumerate(((hr, right), (hl, left))):
            arrived(rb.at[side], recv(side))
            at = pl.ds(pl.multiple_of(to * n + side * half, half), half)
            tx[at, :] = (tx[at, :].astype(F32) + rb[side].astype(F32)).astype(BF16)
            rdma(tx.at[pl.ds(to * n, n), :], rx.at[side], send(2 + side), recv(2 + side), dev)

    def scatter_end(tx, rx, n, recv):
        arrived(rx.at[0], recv(2))
        arrived(rx.at[1], recv(3))
        own = tx[pl.ds(pl.multiple_of(h * n, n), n), :].astype(F32)
        return own + rx[0].astype(F32) + rx[1].astype(F32)

    barrier = pltpu.get_barrier_semaphore()
    count = 0
    for k in range(1, B):
        pl.semaphore_signal(barrier, inc=1, device_id={"blk": lax.rem(b + k, B)}, device_id_type=MESH)
        count += 1
    for k in range(1, T):
        pl.semaphore_signal(barrier, inc=1, device_id={"tensor": lax.rem(t + k, T)}, device_id_type=MESH)
        count += 1
    for k in range(1, U):
        for cc in range(C):
            pl.semaphore_signal(
                barrier, inc=1,
                device_id={"ulysses": lax.rem(u + k, U), "tensor": h * C + cc},
                device_id_type=MESH,
            )
            count += 1

    local = [
        pltpu.make_async_copy(mod_w, mw, loc_sem.at[0]),
        pltpu.make_async_copy(tokens, tok_own, loc_sem.at[1]),
        pltpu.make_async_copy(qkv_w, wq.at[:, c], loc_sem.at[2]),
        pltpu.make_async_copy(out_w, wo.at[c], loc_sem.at[3]),
        pltpu.make_async_copy(up_w, wu.at[c], loc_sem.at[4]),
        pltpu.make_async_copy(down_w, wd.at[c], loc_sem.at[5]),
        pltpu.make_async_copy(cond, cond_v, loc_sem.at[6]),
        pltpu.make_async_copy(q_gain, qg_v, loc_sem.at[7]),
        pltpu.make_async_copy(k_gain, kg_v, loc_sem.at[8]),
    ]
    for copy in local:
        copy.start()

    cf[...] = jnp.zeros_like(cf)
    local[6].wait()
    condf = cond_v[...].astype(F32)
    active = condf * jax.nn.sigmoid(condf)
    active = jnp.concatenate([active[i:i + 1] for i in range(features // 128)], axis=1).astype(BF16)
    local[0].wait()
    share = lax.dot_general(
        jnp.broadcast_to(active, (16, features)), mw[...],
        (((1,), (1,)), ((), ())), preferred_element_type=F32,
    )
    n_share = mod_w.shape[0]
    start = n_share * (b * T + t)
    lanes2 = lax.broadcasted_iota(jnp.int32, (n_share, 256), 1)
    rows2 = lax.broadcasted_iota(jnp.int32, (n_share, 256), 0)
    place = (lanes2 == rows2 + lax.rem(start, 128)).astype(F32)
    placed = jnp.dot(share[0:8], place, preferred_element_type=F32, precision=lax.Precision.HIGHEST)
    sub8 = lax.broadcasted_iota(jnp.int32, (8, 128), 0)
    tile = jnp.where(sub8 == 0, placed[:, 0:128], jnp.where(sub8 == 1, placed[:, 128:256], 0.0))
    m_tx[...] = tile
    m_a[b] = tile

    pl.semaphore_wait(barrier, count)

    for k in range(1, B):
        rdma(m_tx, m_a.at[b], ma_send.at[k], ma_recv.at[b], {"blk": lax.rem(b + k, B)})
    for up_ in range(U):
        rdma_or_local(
            jnp.logical_and(u == up_, c == uc),
            tokens, tok_rx.at[c, pl.ds(ui * R, R), :], tok_send.at[up_], tok_recv.at[c, ui],
            {"ulysses": up_, "tensor": h * C + uc},
        )
    rdma(qkv_w, wq.at[:, c], w_send.at[0], w_recv.at[0], mate)
    rdma(out_w, wo.at[c], w_send.at[1], w_recv.at[1], mate)
    rdma(up_w, wu.at[c], w_send.at[2], w_recv.at[2], mate)
    rdma(down_w, wd.at[c], w_send.at[3], w_recv.at[3], mate)

    per_u = n_share * B * T // 128
    m_d[...] = jnp.zeros_like(m_d)
    for k in range(B):
        if k:
            bp = lax.rem(b + k, B)
            arrived(m_a.at[bp], ma_recv.at[bp])
    for bp in range(B):
        row = (n_share * (bp * T + t)) // 128
        m_d[pl.ds(row, 1), :] += m_a[bp, 0:1, :]
        m_d[pl.ds(row + 1, 1), :] += m_a[bp, 1:2, :]
    m_b[t] = m_d[...]
    for k in range(1, T):
        rdma(m_d, m_b.at[t], mb_send.at[k], mb_recv.at[t], {"tensor": lax.rem(t + k, T)})

    for cc in range(C):
        for i in range(H):
            arrived(tok_rx.at[cc, pl.ds(i * R, R), :], tok_recv.at[cc, i])
    x0 = tok_rx[0].astype(F32)
    x1 = tok_rx[1].astype(F32)
    local_mean = (jnp.sum(x0, -1, keepdims=True) + jnp.sum(x1, -1, keepdims=True)) * (1.0 / (C * W))
    d0 = x0 - local_mean
    d1 = x1 - local_mean
    local_m2 = jnp.sum(d0 * d0, -1, keepdims=True) + jnp.sum(d1 * d1, -1, keepdims=True)
    lane = lax.broadcasted_iota(jnp.int32, (G, 128), 1)
    stats = jnp.where(lane == 0, local_mean, jnp.where(lane == 1, local_m2, 0.0))
    stats_t = jnp.transpose(stats)[0:8]
    st_tx[...] = stats_t
    st_rx[h] = stats_t
    for k in range(1, H):
        hp, dev = y_peer(k)
        rdma(st_tx, st_rx.at[h], st_send.at[k], st_recv.at[h], dev)

    for k in range(1, T):
        tp = lax.rem(t + k, T)
        arrived(m_b.at[tp], mb_recv.at[tp])
    dense = m_b[0]
    for tp in range(1, T):
        dense = dense + m_b[tp]
    m_u[...] = dense
    m_c[u] = dense
    for k in range(1, U):
        rdma(m_u, m_c.at[u], mc_send.at[k], mc_recv.at[u], {"ulysses": lax.rem(u + k, U)})

    for k in range(1, H):
        hp, _ = y_peer(k)
        arrived(st_rx.at[hp], st_recv.at[hp])
    mean = st_rx[0, 0:1, :]
    for hp in range(1, H):
        mean = mean + st_rx[hp, 0:1, :]
    mean = mean * (1.0 / H)
    m2 = jnp.zeros_like(mean)
    for hp in range(H):
        diff = st_rx[hp, 0:1, :] - mean
        m2 = m2 + st_rx[hp, 1:2, :] + (C * W) * diff * diff
    rstd = lax.rsqrt(m2 * (1.0 / features) + 1e-06)
    subg = lax.broadcasted_iota(jnp.int32, (128, G), 0)
    cols = jnp.transpose(jnp.where(subg == 0, mean, jnp.where(subg == 1, rstd, 0.0)))
    mean_c, rstd_c = cols[:, 0:1], cols[:, 1:2]

    for k in range(1, U):
        upk = lax.rem(u + k, U)
        arrived(m_c.at[upk], mc_recv.at[upk])
    for v in range(6):
        for k in range(C * W // 128):
            row = v * (features // 128) + h * (C * W // 128) + k
            modv[v:v + 1, 128 * k:128 * (k + 1)] = m_c[row // per_u, pl.ds(lax.rem(row, per_u), 1), :]

    n0 = ((x0 - mean_c) * rstd_c * (1.0 + modv[1:2, 0:W]) + modv[0:1, 0:W]).astype(BF16)
    n1 = ((x1 - mean_c) * rstd_c * (1.0 + modv[1:2, W:2 * W]) + modv[0:1, W:2 * W]).astype(BF16)

    local[2].wait()
    arrived(wq.at[:, 1 - c], w_recv.at[0])
    def rs_sems(sems, g):
        return lambda k: sems.at[g, k]

    for g in range(3):
        part = jnp.dot(n0, wq[g, 0], preferred_element_type=F32)
        part = part + jnp.dot(n1, wq[g, 1], preferred_element_type=F32)
        rs_tx[g] = part.astype(BF16)
        scatter_start(rs_tx.at[g], rs_rb.at[g], R, rs_sems(rs_send, g), rs_sems(rs_recv, g))

    heads = W // 128

    def proj_relay(g):
        scatter_relay(rs_tx.at[g], rs_rb.at[g], rs_rx.at[g], R, rs_sems(rs_send, g), rs_sems(rs_recv, g))

    def kv_rows(g):
        return lambda hp, lo, n: kv_rx.at[g, pl.ds((c * H + hp) * R + lo, n), :]

    def to_mate(g, hp, i):
        rows = kv_rows(g)(hp, 0, R)
        rdma(rows, rows, km_send.at[g, i], km_recv.at[g, hp], mate)

    def proj_end(g):
        total = scatter_end(rs_tx.at[g], rs_rx.at[g], R, rs_sems(rs_recv, g))
        if g < 2:
            local[7 + g].wait()
            gain = (qg_v if g == 0 else kg_v)[...]
            pieces = []
            for hd in range(heads):
                piece = total[:, 128 * hd:128 * (hd + 1)]
                ms = jnp.mean(piece * piece, axis=-1, keepdims=True)
                pieces.append(piece * lax.rsqrt(ms + 1e-06) * gain)
            total = jnp.concatenate(pieces, axis=1)
        if g == 0:
            for s in range(S):
                q_rx[s, pl.ds(pl.multiple_of(b * N, N), N), :] = total[s * N:(s + 1) * N].astype(BF16)
                rows = q_rx.at[s, pl.ds(b * N, N), :]
                for k in sorted(range(1, B), key=lambda k: -min(k, B - k)):
                    rdma(rows, rows, q_send.at[s, k], q_recv.at[s, b], {"blk": lax.rem(b + k, B)})
        else:
            kv_rx[g - 1, pl.ds(pl.multiple_of((c * H + h) * R, R), R), :] = total.astype(BF16)
            gather_start(kv_rows(g - 1), R, rs_sems(kv_send, g - 1), rs_sems(kv_recv, g - 1))
            to_mate(g - 1, h, 0)

    local[4].wait()
    arrived(wu.at[1 - c], w_recv.at[2])
    for cc in range(C):
        cut = slice(cc * W, (cc + 1) * W)
        vecs = []
        for vec in (1.0 + modv[4:5, cut], modv[3:4, cut]):
            high = vec.astype(BF16).astype(F32)
            vecs += [high, vec - high]
        sub16 = lax.broadcasted_iota(jnp.int32, (16, W), 0)
        left_side = jnp.zeros((16, W), F32)
        for i, vec in enumerate(vecs):
            left_side = jnp.where(sub16 == i, vec, left_side)
        cols16 = jnp.dot(left_side.astype(BF16), wu[cc], preferred_element_type=F32)
        cv_tx[cc:cc + 1, :] = cols16[0:1] + cols16[1:2]
        shifted = cols16[2:3] + cols16[3:4]
        cv_tx[2:3, :] = shifted if cc == 0 else cv_tx[2:3, :] + shifted
    cv_tx[3:8, :] = jnp.zeros((5, wu.shape[2]), F32)
    cv_rx[h] = cv_tx[...]

    proj_relay(0)
    proj_relay(1)
    proj_end(0)
    proj_relay(2)
    proj_end(1)
    proj_end(2)
    for g in range(2):
        gather_relay(kv_rows(g), R, rs_sems(kv_send, g), rs_sems(kv_recv, g))
        to_mate(g, hl, 1)
        to_mate(g, hr, 2)
    for g in range(2):
        gather_end(kv_rows(g), R, rs_sems(kv_recv, g))
        to_mate(g, ho, 3)
    for k in range(1, B):
        bp = lax.rem(b + k, B)
        for s in range(S):
            arrived(q_rx.at[s, pl.ds(bp * N, N), :], q_recv.at[s, bp])
    for g in range(2):
        for hp in range(H):
            arrived(kv_rx.at[g, pl.ds(((1 - c) * H + hp) * R, R), :], km_recv.at[g, hp])

    scale = 1.0 / math.sqrt(128)
    TB = 128 // N
    nq = B // TB
    own_cols = pl.ds(pl.multiple_of(c * W, 128), W)
    J, FW = up_tx.shape[1], up_tx.shape[3]

    def sems(ref, *index):
        return lambda k: ref.at[(*index, k)]

    def to_owners(s, tx, rx, send, recv, cc):
        for hp in range(H):
            up_ = c * H + hp
            rdma_or_local(
                jnp.logical_and(up_ == u, c == cc),
                tx.at[s, cc, pl.ds(hp * N, N), :], rx.at[s, u], send.at[s, cc, hp], recv.at[s, u],
                {"ulysses": up_, "tensor": h * C + cc},
            )

    def from_owners(s, rx, recv):
        for up_ in range(U):
            arrived(rx.at[s, up_], recv.at[s, up_])
        total = rx[s, 0].astype(F32)
        for up_ in range(1, U):
            total = total + rx[s, up_].astype(F32)
        return total

    def fix_copies(s):
        return [
            pltpu.make_async_remote_copy(
                src_ref=fx_tx.at[s], dst_ref=fx_rx.at[s], send_sem=fx_send.at[s, k], recv_sem=fx_recv.at[s],
                device_id={"ulysses": lax.rem(u + k, U)}, device_id_type=MESH,
            )
            for k in range(1, U)
        ]

    def part_steps(s):
        for off in range(nq - 1, -1, -1):
            qb = lax.rem(b // TB + off, nq)
            at = pl.multiple_of(qb * 128, 128)
            lane_q = lax.broadcasted_iota(jnp.int32, (128, 128), 1)
            tail = jnp.zeros((128, 128), F32)
            for hd in range(heads):
                cut = slice(128 * hd, 128 * (hd + 1))
                score = lax.dot_general(
                    q_rx[s, pl.ds(at, 128), cut], kv_rx[0, :, cut],
                    (((1,), (1,)), ((), ())), preferred_element_type=F32,
                )
                top = jnp.max(score, axis=-1, keepdims=True)
                p = jnp.exp((score - top) * scale)
                weight = jnp.sum(p, axis=-1, keepdims=True)
                o = jnp.dot(p.astype(BF16), kv_rx[1, :, cut], preferred_element_type=F32)
                o_tx[s, pl.ds(at, 128), cut] = o.astype(BF16)
                tail = jnp.where(lane_q == hd, top, tail)
                tail = jnp.where(lane_q == heads + hd, weight, tail)
            os_tx[s, qb] = jnp.transpose(tail)[0:8]
            for e in range(TB):
                bp = TB * qb + lax.rem(b + e, TB)
                if off == 0 and e == 0:
                    o_rx[s, b] = o_tx[s, pl.ds(pl.multiple_of(b * N, N), N), :]
                    os_rx[s, b] = os_tx[s, qb]
                    continue
                k, dev = off * TB + e, {"blk": bp}
                rdma(o_tx.at[s, pl.ds(bp * N, N), :], o_rx.at[s, b], o_send.at[s, k], o_recv.at[s, b], dev)
                rdma(os_tx.at[s, qb], os_rx.at[s, b], os_send.at[s, k], os_recv.at[s, b], dev)
        yield

        if s == 0:
            for k in range(1, H):
                _, dev = y_peer(k)
                rdma(cv_tx, cv_rx.at[h], cv_send.at[k], cv_recv.at[h], dev)

        for k in range(1, B):
            bp = lax.rem(b + k, B)
            arrived(os_rx.at[s, bp], os_recv.at[s, bp])
        for hd in range(heads):
            tops = [os_rx[s, bp, hd:hd + 1, :] for bp in range(B)]
            top = functools.reduce(jnp.maximum, tops)
            shares = [jnp.exp((tops[bp] - top) * scale) for bp in range(B)]
            den = shares[0] * os_rx[s, 0, heads + hd:heads + hd + 1, :]
            for bp in range(1, B):
                den = den + shares[bp] * os_rx[s, bp, heads + hd:heads + hd + 1, :]
            for bp in range(B):
                cf[hd * B + bp:hd * B + bp + 1, :] = shares[bp] / den
        cf_t[...] = jnp.transpose(cf[...])
        coef = cf_t[pl.ds(pl.multiple_of(lax.rem(b, TB) * N, N), N), :]
        for k in range(1, B):
            bp = lax.rem(b + k, B)
            arrived(o_rx.at[s, bp], o_recv.at[s, bp])
        pieces = []
        for hd in range(heads):
            cut = slice(128 * hd, 128 * (hd + 1))
            num = coef[:, hd * B:hd * B + 1] * o_rx[s, 0, :, cut].astype(F32)
            for bp in range(1, B):
                num = num + coef[:, hd * B + bp:hd * B + bp + 1] * o_rx[s, bp, :, cut].astype(F32)
            pieces.append(num)

        def ctx_rows(hp, lo, n):
            return ctx_rx.at[s, pl.ds(hp * N + lo, n), :]

        ctx_rx[s, pl.ds(pl.multiple_of(h * N, N), N), :] = jnp.concatenate(pieces, axis=1).astype(BF16)
        gather_start(ctx_rows, N, sems(cx_send, s), sems(cx_recv, s))
        yield
        gather_relay(ctx_rows, N, sems(cx_send, s), sems(cx_recv, s))
        yield
        if s == 0:
            local[3].wait()
            arrived(wo.at[1 - c], w_recv.at[1])
        gather_end(ctx_rows, N, sems(cx_recv, s))

        for cc in range(C):
            at_tx[s, cc] = jnp.dot(ctx_rx[s], wo[cc], preferred_element_type=F32).astype(BF16)
            to_owners(s, at_tx, at_rx, at_send, at_recv, cc)
        yield
        attended = from_owners(s, at_rx, at_recv)
        if s == 0:
            local[1].wait()
        mine = slice(s * N, (s + 1) * N)
        mix[mine, :] = tok_own[mine, :].astype(F32) + modv[2:3, own_cols] * attended
        mixed = mix[mine, :]

        mean_l = jnp.sum(mixed, -1, keepdims=True) * (1.0 / W)
        diff = mixed - mean_l
        n2_tx[s] = (diff * (1.0 + modv[4:5, own_cols])).astype(BF16)
        for up_ in range(U):
            rdma_or_local(
                jnp.logical_and(u == up_, c == uc),
                n2_tx.at[s], n2_rx.at[s, c, pl.ds(ui * N, N), :], n2_send.at[s, up_], n2_recv.at[s, c, ui],
                {"ulysses": up_, "tensor": h * C + uc},
            )
        m2_l = jnp.sum(diff * diff, -1, keepdims=True)
        lane_r = lax.broadcasted_iota(jnp.int32, (N, 128), 1)
        st2 = jnp.where(lane_r == 0, mean_l, jnp.where(lane_r == 1, m2_l, 0.0))
        st2_t = jnp.transpose(jnp.concatenate([st2, jnp.zeros((128 - N, 128), F32)], axis=0))[0:8]
        s2_tx[s] = st2_t
        s2_rx[s, t] = st2_t
        for k in range(1, T):
            rdma(s2_tx.at[s], s2_rx.at[s, t], s2_send.at[s, k], s2_recv.at[s, t], {"tensor": lax.rem(t + k, T)})
        yield
        for cc in range(C):
            for i in range(H):
                arrived(n2_rx.at[s, cc, pl.ds(i * N, N), :], n2_recv.at[s, cc, i])

        def act_rows(j):
            return lambda hp, lo, n: act_rx.at[s, j, pl.ds(hp * N + lo, n), :]

        for j in range(J):
            cut = slice(FW * j, FW * (j + 1))
            part = jnp.dot(n2_rx[s, 0], wu[0, :, cut], preferred_element_type=F32)
            part = part + jnp.dot(n2_rx[s, 1], wu[1, :, cut], preferred_element_type=F32)
            up_tx[s, j] = part.astype(BF16)
            scatter_start(up_tx.at[s, j], up_rb.at[s, j], N, sems(up_send, s, j), sems(up_recv, s, j))
        yield
        for k in range(1, T):
            tp = lax.rem(t + k, T)
            arrived(s2_rx.at[s, tp], s2_recv.at[s, tp])
        total = s2_rx[s, 0]
        for tp in range(1, T):
            total = total + s2_rx[s, tp]
        mean2 = total[0:1] * (1.0 / T)
        m2 = total[1:2]
        for tp in range(T):
            dev2 = s2_rx[s, tp, 0:1, :] - mean2
            m2 = m2 + W * dev2 * dev2
            fx_tx[s, tp:tp + 1, :] = dev2
        fx_tx[s, T:T + 1, :] = lax.rsqrt(m2 * (1.0 / features) + 1e-06)
        fx_tx[s, T + 1:16, :] = jnp.zeros((16 - T - 1, 128), F32)
        sends = u == c * H + h

        @pl.when(sends)
        def _():
            fx_rx[s] = fx_tx[s]
            for copy in fix_copies(s):
                copy.start()

        yield
        for j in range(J):
            scatter_relay(
                up_tx.at[s, j], up_rb.at[s, j], up_rx.at[s, j], N, sems(up_send, s, j), sems(up_recv, s, j)
            )
            yield
        for j in range(J):
            hidden = scatter_end(up_tx.at[s, j], up_rx.at[s, j], N, sems(up_recv, s, j))
            if j == 0:

                @pl.when(u != c * H + h)
                def _():
                    arrived(fx_rx.at[s], fx_recv.at[s])

                if s == 0:
                    for k in range(1, H):
                        hp, _ = y_peer(k)
                        arrived(cv_rx.at[hp], cv_recv.at[hp])
                fix = jnp.transpose(jnp.concatenate([fx_rx[s], jnp.zeros((112, 128), F32)], axis=0))[0:N]
            cut = slice(FW * j, FW * (j + 1))
            shifted = cv_rx[0, 2:3, cut]
            for hp in range(1, H):
                shifted = shifted + cv_rx[hp, 2:3, cut]
            for tp in range(T):
                hidden = hidden + fix[:, tp:tp + 1] * cv_rx[tp // C, tp % C:tp % C + 1, cut]
            hidden = fix[:, T:T + 1] * hidden + shifted
            act_rx[s, j, pl.ds(pl.multiple_of(h * N, N), N), :] = jax.nn.gelu(hidden, approximate=True).astype(BF16)
            gather_start(act_rows(j), N, sems(ac_send, s, j), sems(ac_recv, s, j))
            yield
        for j in range(J):
            gather_relay(act_rows(j), N, sems(ac_send, s, j), sems(ac_recv, s, j))
            yield
        if s == 0:
            local[5].wait()
            arrived(wd.at[1 - c], w_recv.at[3])
        accs = [None] * C
        for j in range(J):
            gather_end(act_rows(j), N, sems(ac_recv, s, j))
            for cc in range(C):
                part = jnp.dot(act_rx[s, j], wd[cc, FW * j:FW * (j + 1), :], preferred_element_type=F32)
                accs[cc] = part if j == 0 else accs[cc] + part
                if j == J - 1:
                    ff_tx[s, cc] = accs[cc].astype(BF16)
                    to_owners(s, ff_tx, ff_rx, ff_send, ff_recv, cc)
            yield
        feed = from_owners(s, ff_rx, ff_recv)
        out[mine, :] = mix[mine, :] + modv[5:6, own_cols] * feed

    steps = [part_steps(s) for s in range(S)]
    for s in ORDER:
        next(steps[s], None)

    for s in range(S):

        @pl.when(u == c * H + h)
        def _():
            for copy in fix_copies(s):
                copy.wait_send()

    for own, copy in pending:
        if own is None:
            copy.wait_send()
        else:
            pl.when(jnp.logical_not(own))(copy.wait_send)


def on_device(
    tokens, cond, mod_weight, qkv_weight, q_gain, k_gain, out_weight, up_weight, down_weight
):
    U = lax.axis_size("ulysses")
    B = lax.axis_size("blk")
    T = lax.axis_size("tensor")
    H = T // 2
    R, W = tokens.shape
    G = H * R
    FFL = up_weight.shape[1]
    J = 2
    S = 2
    N = R // S
    dma = pltpu.SemaphoreType.DMA
    vmem = pltpu.VMEM
    any_spec = pl.BlockSpec(memory_space=pltpu.HBM)
    vm_spec = pl.BlockSpec(memory_space=pltpu.VMEM)
    return pl.pallas_call(
        functools.partial(block_kernel, U, B, T),
        out_shape=jax.ShapeDtypeStruct((R, W), F32),
        in_specs=[any_spec] * 9,
        out_specs=vm_spec,
        scratch_shapes=[
            vmem((R, W), BF16),
            vmem((mod_weight.shape[0] // 128, 128), BF16),
            vmem((1, 128), F32),
            vmem((1, 128), F32),
            vmem((2, G, W), BF16),
            vmem((mod_weight.shape[1], mod_weight.shape[0]), BF16),
            vmem((3, 2, W, W), BF16),
            vmem((2, W, W), BF16),
            vmem((2, W, FFL), BF16),
            vmem((2, FFL, W), BF16),
            vmem((8, 128), F32),
            vmem((B, 8, 128), F32),
            vmem((24, 128), F32),
            vmem((T, 24, 128), F32),
            vmem((24, 128), F32),
            vmem((U, 24, 128), F32),
            vmem((8, 2 * W), F32),
            vmem((8, G), F32),
            vmem((H, 8, G), F32),
            vmem((3, G, W), BF16),
            vmem((3, 2, R // 2, W), BF16),
            vmem((3, 2, R, W), BF16),
            vmem((S, B * N, W), BF16),
            vmem((2, T * R, W), BF16),
            vmem((S, B * N, W), BF16),
            vmem((S, B, N, W), BF16),
            vmem((S, B * N // 128, 8, 128), F32),
            vmem((S, B, 8, 128), F32),
            vmem((128, 128), F32),
            vmem((128, 128), F32),
            vmem((S, H * N, W), BF16),
            vmem((S, 2, H * N, W), BF16),
            vmem((S, U, N, W), BF16),
            vmem((R, W), F32),
            vmem((S, 8, 128), F32),
            vmem((S, T, 8, 128), F32),
            vmem((S, 16, 128), F32),
            vmem((S, 16, 128), F32),
            vmem((8, FFL), F32),
            vmem((H, 8, FFL), F32),
            vmem((S, N, W), BF16),
            vmem((S, 2, H * N, W), BF16),
            vmem((S, J, H * N, FFL // J), BF16),
            vmem((S, J, 2, N // 2, FFL // J), BF16),
            vmem((S, J, 2, N, FFL // J), BF16),
            vmem((S, J, H * N, FFL // J), BF16),
            vmem((S, 2, H * N, W), BF16),
            vmem((S, U, N, W), BF16),
            dma((9,)), dma((4,)), dma((4,)),
            dma((U,)), dma((2, H)), dma((B,)), dma((B,)), dma((T,)), dma((T,)), dma((U,)), dma((U,)),
            dma((H,)), dma((H,)), dma((3, H)), dma((3, H)), dma((S, B)), dma((S, B)),
            dma((2, H)), dma((2, H)), dma((2, H)), dma((2, H)), dma((S, B)), dma((S, B)), dma((S, B)), dma((S, B)),
            dma((S, H)), dma((S, H)), dma((S, 2, H)), dma((S, U)), dma((S, T)), dma((S, T)), dma((S, U)), dma((S,)), dma((H,)), dma((H,)), dma((S, U)), dma((S, 2, H)),
            dma((S, J, H)), dma((S, J, H)), dma((S, J, H)), dma((S, J, H)), dma((S, 2, H)), dma((S, U)),
        ],
        compiler_params=pltpu.CompilerParams(
            collective_id=0, has_side_effects=True, vmem_limit_bytes=67043328
        ),
        name="block_kernel",
    )(
        tokens,
        cond.reshape(-1, 128),
        mod_weight.T,
        qkv_weight.transpose(1, 0, 2),
        q_gain.reshape(1, -1),
        k_gain.reshape(1, -1),
        out_weight,
        up_weight,
        down_weight,
    )


def solution(mesh):
    return jax.shard_map(
        on_device,
        mesh=mesh,
        in_specs=(
            P(("ulysses", "blk"), "tensor"),
            P(),
            P(None, ("ulysses", "blk", "tensor")),
            P("tensor", None, "ulysses"),
            P(),
            P(),
            P("ulysses", "tensor"),
            P("tensor", "ulysses"),
            P("ulysses", "tensor"),
        ),
        out_specs=P(("ulysses", "blk"), "tensor"),
        check_vma=False,
    )
```
